32 devices in a mesh: lat: 2 (over x), lon: 8 (over z, y), grp: 2 (over core).
Axes of the slice: x: 2, y: 2, z: 4, core: 2. Of those that a mesh axis runs over, the one named last changes fastest.
Arguments:
- teacher_in: bfloat16 [2, 48, 96, 512], P('grp', 'lat', 'lon'), may hold values from -6 to 6
- student_in: bfloat16 [2, 48, 96, 256], P('grp', 'lat', 'lon'), may hold values from -6 to 6
- regions: int32 [2, 48, 96], P(None, 'lat', 'lon'), may hold values from 0 to 2
- t_qkv: bfloat16 [2, 512, 1536], replicated, may hold values from -0.25 to 0.25
- t_out: bfloat16 [2, 512, 512], replicated, may hold values from -0.25 to 0.25
- s_qkv: bfloat16 [2, 256, 768], replicated, may hold values from -0.375 to 0.375
- s_out: bfloat16 [2, 256, 256], replicated, may hold values from -0.375 to 0.375
- s_proj: bfloat16 [256, 512], replicated, may hold values from -0.375 to 0.375
Outputs:
- teacher_out: bfloat16 [2, 48, 96, 512], P('grp', 'lat', 'lon')
- student_grad: float32 [2, 48, 96, 256], P('grp', 'lat', 'lon')
The draws below stay inside these ranges and needn't reach their ends.
All inputs are finite; a program needn't handle non-finite values.
Results may differ from the reference program's by a relative error of at most 0.02.
Values may be sent and summed in bfloat16 or wider, within the bound.
A program may use at most 128 MiB of HBM per device.

```python
import jax
import jax.numpy as jnp
from jax import lax

D_T = 512
HEADS_T = 8
D_S = 256
HEADS_S = 4
LEV = 2
LAYERS = 2
LAT = 48
LON = 96


def place_ends(drawn, stream_key, smallest, top_value):
    spot = [jax.random.randint(jax.random.fold_in(stream_key, axis), (), 0, length) for axis, length in enumerate(drawn.shape)]
    main_axis = drawn.shape.index(max(drawn.shape))
    next_to = spot[:main_axis] + [(spot[main_axis] + 1) % drawn.shape[main_axis]] + spot[main_axis + 1:]
    return drawn.at[tuple(spot)].set(smallest).at[tuple(next_to)].set(top_value)


def level_of(stream_key, dims, cuts, low, largest):
    factor_of = 1.0
    for position, parts in cuts:
        steps = jax.random.uniform(jax.random.fold_in(jax.random.fold_in(stream_key, 6), position), (parts,), jnp.float32, low / len(cuts), largest / len(cuts))
        factor_of = factor_of * jnp.repeat(jnp.exp(steps), dims[position] // parts).reshape((-1,) + (1,) * (len(dims) - 1 - position))
    return factor_of


def centred(stream_key, dims, deviation, bound, pieces=(), kind=jnp.bfloat16):
    factor_of = level_of(stream_key, dims, pieces, -0.22, 0.18) if pieces else 1.0
    values = jax.random.normal(stream_key, dims, jnp.float32) * deviation * factor_of
    return jnp.minimum(jnp.maximum(values, -bound), bound).astype(kind)


def setup_inputs(seed: int = 0) -> dict:
    keys = jax.random.split(jax.random.key(seed), 9)
    return {
        "teacher_in": centred(keys[0], (LEV, LAT, LON, D_T), 1.0, 6.0, ((0, 2), (1, 2), (2, 8))),
        "student_in": centred(keys[1], (LEV, LAT, LON, D_S), 1.0, 6.0, ((0, 2), (1, 2), (2, 8))),
        "regions": place_ends(jax.random.randint(keys[2], (LEV, LAT, LON), 0, 3), jax.random.fold_in(keys[2], 1), 0, 2).astype(jnp.int32),
        "t_qkv": centred(keys[3], (LAYERS, D_T, 3 * D_T), D_T ** -0.5, 0.25),
        "t_out": centred(keys[4], (LAYERS, D_T, D_T), D_T ** -0.5, 0.25),
        "s_qkv": centred(keys[5], (LAYERS, D_S, 3 * D_S), D_S ** -0.5, 0.375),
        "s_out": centred(keys[6], (LAYERS, D_S, D_S), D_S ** -0.5, 0.375),
        "s_proj": centred(keys[7], (D_S, D_T), D_S ** -0.5, 0.375),
    }


logit_scale = 10.0
eps = 1e-06

def windows(source, win_rows, win_cols):
    levels, height, breadth = (source.shape[0], source.shape[1], source.shape[2])
    trailing = source.shape[3:]
    shaped = source.reshape((levels, height // win_rows, win_rows, breadth // win_cols, win_cols) + trailing)
    permute = (1, 3, 0, 2, 4) + tuple(range(5, 5 + len(trailing)))
    shaped = shaped.transpose(permute)
    return shaped.reshape((height // win_rows * (breadth // win_cols), levels * win_rows * win_cols) + trailing)

def unwindows(windowed, levels, height, breadth, win_rows, win_cols):
    trailing = windowed.shape[2:]
    shaped = windowed.reshape((height // win_rows, breadth // win_cols, levels, win_rows, win_cols) + trailing)
    permute = (2, 0, 3, 1, 4) + tuple(range(5, 5 + len(trailing)))
    return shaped.transpose(permute).reshape((levels, height, breadth) + trailing)

def attend(queries, key_rows, value_rows, reg_query, reg_key, head_count):
    nwin, nquery, channels = queries.shape
    nkey = key_rows.shape[1]
    head_size = channels // head_count
    q_heads = queries.reshape(nwin, nquery, head_count, head_size).astype(jnp.float32)
    k_heads = key_rows.reshape(nwin, nkey, head_count, head_size).astype(jnp.float32)
    v_heads = value_rows.reshape(nwin, nkey, head_count, head_size).astype(jnp.float32)
    products = jnp.einsum('wqhd,wkhd->whqk', q_heads, k_heads)
    query_sq = lax.optimization_barrier(jnp.sum(q_heads * q_heads, axis=3))
    key_sq = lax.optimization_barrier(jnp.sum(k_heads * k_heads, axis=3))
    scale_q = lax.rsqrt(query_sq + eps).transpose(0, 2, 1)[:, :, :, None]
    scale_k = lax.rsqrt(key_sq + eps).transpose(0, 2, 1)[:, :, None, :]
    scores = logit_scale * products * scale_q * scale_k
    allowed = reg_query[:, :, None] == reg_key[:, None, :]
    exponent = jnp.where(allowed[:, None], jnp.exp(scores), jnp.zeros((), jnp.float32))
    denominator = lax.optimization_barrier(jnp.sum(exponent, axis=3, keepdims=True))
    weights = (exponent / jnp.where(denominator > 0, denominator, jnp.ones((), jnp.float32))).astype(jnp.bfloat16)
    blended = jnp.einsum('whqk,wkhd->wqhd', weights.astype(jnp.float32), v_heads)
    return blended.astype(jnp.bfloat16).reshape(nwin, nquery, channels)

def project(source, matrix):
    channels = source.shape[-1]
    flat = source.reshape(-1, channels).astype(jnp.bfloat16)
    result = jnp.dot(flat, matrix, preferred_element_type=jnp.float32).astype(jnp.bfloat16)
    return result.reshape(source.shape[:-1] + (matrix.shape[1],))

def finish(source, attended, w_output):
    channels = source.shape[-1]
    output = jnp.dot(attended.reshape(-1, channels), w_output, preferred_element_type=jnp.float32)
    normed = output * lax.rsqrt(lax.optimization_barrier(jnp.mean(output * output, axis=-1, keepdims=True)) + eps)
    return (source.reshape(-1, channels).astype(jnp.float32) + normed).astype(jnp.bfloat16).reshape(source.shape)

def student_grad(student_in, reg_own, target, s_qkv, s_out, s_proj, head_count):
    levels, height, breadth, channels = student_in.shape
    reg_win = windows(reg_own.reshape(1, levels * height, breadth), 12, 6)

    def loss_fn(inputs):
        hidden = inputs
        for layer_idx in range(s_qkv.shape[0]):
            projected = project(hidden, s_qkv[layer_idx]).reshape(1, levels * height, breadth, 3 * channels)
            queries = windows(projected[..., :channels], 12, 6)
            key_rows = windows(projected[..., channels:2 * channels], 12, 6)
            value_rows = windows(projected[..., 2 * channels:], 12, 6)
            attended = attend(queries, key_rows, value_rows, reg_win, reg_win, head_count)
            attended = unwindows(attended, 1, levels * height, breadth, 12, 6).reshape(levels, height, breadth, channels)
            hidden = finish(hidden, attended, s_out[layer_idx])
        predicted = jnp.dot(hidden.reshape(-1, channels), s_proj, preferred_element_type=jnp.float32)
        residual = predicted - target.reshape(-1, target.shape[-1]).astype(jnp.float32)
        return 0.5 * jnp.sum(residual * residual)
    loss_value, pullback = jax.vjp(loss_fn, student_in.astype(jnp.float32))
    return pullback(jnp.ones((), jnp.float32))[0]

def place(source, filler):
    rolled = jnp.roll(source, 3, axis=2)
    widths = ((0, 0), (6, 6), (0, 0)) + ((0, 0),) * (source.ndim - 3)
    return jnp.pad(rolled, widths, constant_values=filler)

def reference(teacher_in, student_in, regions, t_qkv, t_out, s_qkv, s_out, s_proj):
    levels, height, breadth, channels = teacher_in.shape
    projected = project(teacher_in, t_qkv[0])
    queries = windows(projected[..., :channels], 12, 6)
    key_rows = windows(projected[..., channels:2 * channels], 12, 6)
    value_rows = windows(projected[..., 2 * channels:], 12, 6)
    reg_win = windows(regions, 12, 6)
    attended = attend(queries, key_rows, value_rows, reg_win, reg_win, HEADS_T)
    attended = unwindows(attended, levels, height, breadth, 12, 6)
    hidden_a = finish(teacher_in, attended, t_out[0])
    projected = project(hidden_a, t_qkv[1])
    tall = height + 12
    placed = place(projected, 0.0).reshape(1, levels * tall, breadth, 3 * channels)
    reg_placed = place(regions, -1).reshape(1, levels * tall, breadth)
    queries = windows(placed[..., :channels], 12, 6)
    key_rows = windows(placed[..., channels:2 * channels], 12, 6)
    value_rows = windows(placed[..., 2 * channels:], 12, 6)
    reg_win = windows(reg_placed, 12, 6)
    attended = attend(queries, key_rows, value_rows, reg_win, reg_win, HEADS_T)
    attended = unwindows(attended, 1, levels * tall, breadth, 12, 6).reshape(levels, tall, breadth, channels)
    attended = jnp.roll(attended[:, 6:6 + height], -3, axis=2)
    teacher_out = finish(hidden_a, attended, t_out[1])
    gradient = student_grad(student_in, regions, teacher_out, s_qkv, s_out, s_proj, HEADS_S)
    return (teacher_out, gradient)
```

```python
import functools

import jax
import jax.numpy as jnp
import numpy as np
from jax import lax
from jax.experimental import pallas as pl
from jax.experimental.pallas import tpu as pltpu
from jax.sharding import PartitionSpec as P

HEADS_T = 8
HEADS_S = 4
SCALE = 10.0
EPS = 1e-06
BF = jnp.bfloat16
F32 = jnp.float32
MESH = pl.DeviceIdType.MESH

ROWS, COLS = 24, 12
TOK = ROWS * COLS
GROUP = 6 * ROWS
EDGE = 80
KEYS = 3 * EDGE
HALO = 5 * EDGE
FEAT = 128
LOG2E = 1.4426950408889634
MISS = 512.0
SEC_T, SEC_B, SEC_TL, SEC_BL, SEC_TR, SEC_BR = (
    (0, 80),
    (80, 80),
    (160, 32),
    (192, 32),
    (224, 32),
    (256, 32),
)
PACK = 288
K1_VMEM = 32 * 1024 * 1024
K2_VMEM = 32 * 1024 * 1024


def dot(a, b):
    return jnp.dot(a, b, preferred_element_type=F32)


def dot_nt(a, b):
    return lax.dot_general(a, b, (((1,), (1,)), ((), ())), preferred_element_type=F32)


def dot_tn(a, b):
    return lax.dot_general(a, b, (((0,), (0,)), ((), ())), preferred_element_type=F32)


def constants():
    gather = np.zeros((PACK, TOK), np.float32)

    def put(section, cols, rows):
        at = section[0]
        for col in cols:
            for row in rows:
                gather[at, col * ROWS + row] = 1
                at += 1

    top, bottom = range(6), range(ROWS - 6, ROWS)
    first, last = range(3), range(COLS - 3, COLS)
    put(SEC_T, range(COLS), bottom)
    put(SEC_B, range(COLS), top)
    put(SEC_TL, last, bottom)
    put(SEC_BL, last, top)
    put(SEC_TR, first, bottom)
    put(SEC_BR, first, top)
    spread = np.zeros((3 * EDGE, PACK), np.float32)
    for group in range(3):
        for place in range(6):
            col = group * 6 + place - 3
            for end, (mid, before, after) in enumerate(
                ((SEC_T, SEC_TL, SEC_TR), (SEC_B, SEC_BL, SEC_BR))
            ):
                if col < 0:
                    source = before[0] + (col + 3) * 6
                elif col >= COLS:
                    source = after[0] + (col - COLS) * 6
                else:
                    source = mid[0] + col * 6
                for row in range(6):
                    spread[group * EDGE + end * 36 + place * 6 + row, source + row] = 1
    token = np.arange(TOK)[:, None]
    lane = np.arange(FEAT)[None, :]
    marks = np.concatenate(
        [
            token // ROWS == lane,
            token % ROWS == lane,
            16 + token % ROWS // 12 == lane,
            16 + (token % ROWS + 6) // 12 == lane,
        ]
    ).astype(np.float32)
    heads = (np.arange(256)[:, None] // 64 == np.arange(256)[None, :] // 64).astype(np.float32)
    return tuple(jnp.asarray(table, BF) for table in (gather, spread, marks, heads))


def inverse_norm(values, heads):
    square = (values * values).astype(BF)
    parts = [
        dot(square[:, at : at + 256], heads) for at in range(0, values.shape[1], 256)
    ]
    total = parts[0] if len(parts) == 1 else jnp.concatenate(parts, axis=1)
    return lax.rsqrt(total + EPS)


def pair_masks():
    lane = lax.broadcasted_iota(jnp.int32, (1, FEAT), 1)
    low = jnp.where(lane < 64, 1.0, 0.0).astype(F32)
    return low.astype(BF), (1.0 - low).astype(BF)


def wide(left, right):
    return jnp.concatenate([left, jnp.broadcast_to(right, left.shape)], axis=1)


def attend_pair(q, k, v, f_query, f_key):
    query = wide(q, f_query)
    total = None
    for mask in pair_masks():
        exps = jnp.exp2(dot_nt(query, wide(k * mask, f_key))).astype(BF)
        part = dot(exps, wide(v * mask, mask))
        total = part if total is None else total + part
    inverse = 1.0 / total[:, FEAT:]
    return total[:, :FEAT] * inverse, inverse


def lanes(pair):
    return pl.ds(pl.multiple_of(pair * 128, 128), 128)


def rows_of(group):
    return slice(group * GROUP, (group + 1) * GROUP)


def normed(o):
    return lax.rsqrt(jnp.mean(o * o, axis=-1, keepdims=True) + EPS)


def forward_kernel(n_lat, n_lon, *refs):
    (
        x_hbm, s_hbm, reg_hbm, tqkv_hbm, tout_hbm, sqkv_hbm, sout_hbm, sproj_hbm,
        gather_hbm, spread_hbm, marks_hbm, heads_hbm,
        att, hid_t, pred, o_s, rq_s, rk_s, rd_s, q_s, k_s, v_s, att_s, exps_s,
        tout_b, sqkv, sout, sproj, heads,
        x_ref, s_ref, reg_ref, tqkv, tout_a, gather, spread, marks,
        reg_pad, x_far, qa, ka, va, f_qa, f_ka, hid, pack, edge_in, halo, kb, vb, f_kb,
        load, send, recv,
    ) = refs
    lat, lon, grp = lax.axis_index("lat"), lax.axis_index("lon"), lax.axis_index("grp")
    right, left = lax.rem(lon + 1, n_lon), lax.rem(lon + n_lon - 1, n_lon)
    has_up, has_down = lat > 0, lat < n_lat - 1
    barrier = pltpu.get_barrier_semaphore()

    def greet(device):
        pl.semaphore_signal(barrier, inc=1, device_id=device, device_id_type=MESH)

    greet((lat, lon, 1 - grp))
    greet((lat, left, grp))
    greet((lat, right, grp))

    @pl.when(has_up)
    def _():
        for column in (left, lon, right):
            greet((lat - 1, column, grp))

    @pl.when(has_down)
    def _():
        for column in (left, lon, right):
            greet((lat + 1, column, grp))

    moves = dict(
        reg=(reg_hbm, reg_ref),
        marks=(marks_hbm, marks),
        s=(s_hbm, s_ref),
        sqkv=(sqkv_hbm, sqkv),
        heads=(heads_hbm, heads),
        sout=(sout_hbm, sout),
        x=(x_hbm, x_ref),
        qkv_a=(tqkv_hbm.at[0], tqkv.at[0]),
        tout_a=(tout_hbm.at[0], tout_a),
        gather=(gather_hbm, gather),
        qkv_b=(tqkv_hbm.at[1], tqkv.at[1]),
        sproj=(sproj_hbm, sproj),
        spread=(spread_hbm, spread),
        tout_b=(tout_hbm.at[1], tout_b),
    )
    loads = {
        name: pltpu.make_async_copy(source, target, load.at[slot])
        for slot, (name, (source, target)) in enumerate(moves.items())
    }
    for copy in loads.values():
        copy.start()

    @pl.when(jnp.logical_not(has_up))
    def _():
        for at, size in (SEC_T, SEC_TL, SEC_TR):
            edge_in[at : at + size, :] = jnp.zeros((size, 640), BF)

    @pl.when(jnp.logical_not(has_down))
    def _():
        for at, size in (SEC_B, SEC_BL, SEC_BR):
            edge_in[at : at + size, :] = jnp.zeros((size, 640), BF)

    reg_pad[...] = jnp.zeros_like(reg_pad)
    loads["reg"].wait()
    loads["marks"].wait()
    lane = lax.broadcasted_iota(jnp.int32, (TOK, FEAT), 1).astype(F32)
    levels = (reg_ref[:, 0, :], reg_ref[:, 1, :])
    window_a = marks[2 * TOK : 3 * TOK, :]
    for side, (one, two) in enumerate((levels, levels[::-1])):
        reg_pad[0:COLS, 0:ROWS] = jnp.where(grp == 0, one, two).astype(F32)
        region = jnp.sum(
            dot(marks[0:TOK, :], reg_pad[...].astype(BF))
            * marks[TOK : 2 * TOK, :].astype(F32),
            axis=1,
            keepdims=True,
        )
        hot = jnp.where(region == lane, 1.0, 0.0).astype(BF)
        feature = hot + window_a
        f_ka[side] = (feature - 1) * MISS
        if side == 0:
            f_qa[...] = feature
            hid_t[:, 512:640] = hot + marks[3 * TOK : 4 * TOK, :]

    def student_forward(layer, source_ref):
        source = source_ref[...]
        w = sqkv.at[layer]
        q = dot(source, w[:, 0:256]).astype(BF).astype(F32)
        rq = inverse_norm(q, heads[...])
        rq_s[layer] = rq
        q_s[layer] = (q * (rq * (SCALE * LOG2E))).astype(BF)
        k = dot(source, w[:, 256:512]).astype(BF).astype(F32)
        rk = inverse_norm(k, heads[...])
        rk_s[layer] = rk
        k_s[layer] = (k * rk).astype(BF)
        v_s[layer] = dot(source, w[:, 512:768]).astype(BF)
        for pair in range(2):
            cut = slice(pair * 128, pair * 128 + 128)
            for group in range(2):
                rows = rows_of(group)
                out, inverse = attend_pair(
                    q_s[layer, rows, cut],
                    k_s[layer, rows, cut],
                    v_s[layer, rows, cut],
                    f_qa[rows, :],
                    f_ka[0, rows, :],
                )
                att_s[layer, rows, cut] = out.astype(BF)
                rd_s[layer, rows, cut] = inverse
        o = dot(att_s[layer], sout[layer])
        o_s[layer] = o
        return (source.astype(F32) + o * normed(o)).astype(BF)

    def keep_exps(layer):
        for pair in range(2):
            cut = slice(pair * 128, pair * 128 + 128)
            for group in range(2):
                rows = rows_of(group)
                query = wide(q_s[layer, rows, cut], f_qa[rows, :])
                for half, mask in enumerate(pair_masks()):
                    keys = wide(k_s[layer, rows, cut] * mask, f_ka[0, rows, :])
                    exps_s[layer * 4 + pair * 2 + half, rows, :] = jnp.exp2(
                        dot_nt(keys, query)
                    ).astype(BF)

    for name in ("s", "sqkv", "heads", "sout"):
        loads[name].wait()
    hid[...] = student_forward(0, s_ref)

    rows_near = has_up.astype(jnp.int32) + has_down.astype(jnp.int32)
    pl.semaphore_wait(barrier, 3 + 3 * rows_near)

    def copy_to(source, target, slot, device):
        return pltpu.make_async_remote_copy(
            src_ref=source,
            dst_ref=target,
            send_sem=send.at[slot],
            recv_sem=recv.at[slot],
            device_id=device,
            device_id_type=MESH,
        )

    loads["x"].wait()
    to_partner = copy_to(x_ref, x_far, 0, (lat, lon, 1 - grp))
    to_partner.start()

    def keys_of(value, weight):
        keys = dot(value, weight[:, 512:1024]).astype(BF).astype(F32)
        return (keys * inverse_norm(keys, heads[...])).astype(BF)

    def values_of(value, weight):
        return dot(value, weight[:, 1024:1536]).astype(BF)

    def queries_of(value, weight):
        q = dot(value, weight[:, 0:512]).astype(BF).astype(F32)
        return (q * (inverse_norm(q, heads[...]) * (SCALE * LOG2E))).astype(BF)

    loads["qkv_a"].wait()
    w_a = tqkv.at[0]
    qa[...] = queries_of(x_ref[...], w_a)
    ka[0] = keys_of(x_ref[...], w_a)
    va[0] = values_of(x_ref[...], w_a)
    keep_exps(0)
    to_partner.wait()
    ka[1] = keys_of(x_far[...], w_a)
    va[1] = values_of(x_far[...], w_a)

    for group in range(2):
        rows = rows_of(group)
        f_key = jnp.concatenate([f_ka[0, rows, :], f_ka[1, rows, :]], axis=0)

        def pair_a(pair, inner, rows=rows, f_key=f_key):
            cut = lanes(pair)
            out, _ = attend_pair(
                qa[rows, cut],
                jnp.concatenate([ka[0, rows, cut], ka[1, rows, cut]], axis=0),
                jnp.concatenate([va[0, rows, cut], va[1, rows, cut]], axis=0),
                f_qa[rows, :],
                f_key,
            )
            att[rows, cut] = out.astype(BF)
            return inner

        lax.fori_loop(0, 4, pair_a, 0, unroll=True)
    loads["tout_a"].wait()
    o = dot(att[...], tout_a[...])
    hid_t[:, 0:512] = (x_ref[...].astype(F32) + o * normed(o)).astype(BF)

    to_right = copy_to(hid_t.at[TOK - EDGE : TOK], halo.at[0:EDGE], 1, (lat, right, grp))
    to_left = copy_to(hid_t.at[0:EDGE], halo.at[EDGE : 2 * EDGE], 2, (lat, left, grp))
    to_right.start()
    to_left.start()
    loads["gather"].wait()
    pack[...] = dot(gather[...], hid_t[...]).astype(BF)

    def section(sec, slot, device):
        piece = pl.ds(sec[0], sec[1])
        return copy_to(pack.at[piece], edge_in.at[piece], slot, device)

    ups = (
        section(SEC_B, 3, (lat - 1, lon, grp)),
        section(SEC_BL, 4, (lat - 1, right, grp)),
        section(SEC_BR, 5, (lat - 1, left, grp)),
    )
    downs = (
        section(SEC_T, 6, (lat + 1, lon, grp)),
        section(SEC_TL, 7, (lat + 1, right, grp)),
        section(SEC_TR, 8, (lat + 1, left, grp)),
    )

    @pl.when(has_up)
    def _():
        for copy in ups:
            copy.start()

    @pl.when(has_down)
    def _():
        for copy in downs:
            copy.start()

    place = lax.broadcasted_iota(jnp.int32, (EDGE, FEAT), 0)
    after, before = place >= 8, place < EDGE - 8

    def miss(feature, keep=None):
        feature = feature.astype(F32)
        if keep is not None:
            feature = jnp.where(keep, feature, 0.0)
        return ((feature - 1.0) * MISS).astype(BF)

    own = hid_t[:, 512:640]
    f_kb[EDGE : 2 * EDGE, :] = miss(own[0:EDGE], before)
    f_kb[KEYS : KEYS + EDGE, :] = miss(own[64 : 64 + EDGE], after)
    f_kb[KEYS + EDGE : KEYS + 2 * EDGE, :] = miss(own[64 + EDGE : 64 + 2 * EDGE], before)
    f_kb[2 * KEYS : 2 * KEYS + EDGE, :] = miss(own[TOK - EDGE :], after)

    loads["qkv_b"].wait()
    w_b = tqkv.at[1]
    qa[...] = queries_of(hid_t[:, 0:512], w_b)
    for ref, value in (
        (kb, keys_of(hid_t[:, 0:512], w_b)),
        (vb, values_of(hid_t[:, 0:512], w_b)),
    ):
        ref[EDGE : 2 * EDGE, :] = value[0:EDGE]
        ref[KEYS : KEYS + 2 * EDGE, :] = value[64 : 64 + 2 * EDGE]
        ref[2 * KEYS : 2 * KEYS + EDGE, :] = value[TOK - EDGE :]

    last = student_forward(1, hid)
    loads["sproj"].wait()
    pred[...] = dot(last, sproj[...])
    keep_exps(1)
    loads["spread"].wait()
    loads["tout_b"].wait()

    to_right.wait()
    to_left.wait()

    @pl.when(has_up)
    def _():
        for copy in ups:
            copy.wait_send()
        for copy in downs:
            copy.wait_recv()

    @pl.when(has_down)
    def _():
        for copy in downs:
            copy.wait_send()
        for copy in ups:
            copy.wait_recv()

    halo[2 * EDGE :, :] = dot(spread[...], edge_in[...]).astype(BF)
    column = lax.broadcasted_iota(jnp.int32, (EDGE, FEAT), 1)
    window_b = jnp.where(place < 36, 16, jnp.where(place < 72, 18, FEAT))
    ends = jnp.where(column == window_b, 1.0, 0.0)
    f_kb[0:EDGE, :] = miss(halo[0:EDGE, 512:640], after)
    f_kb[2 * KEYS + EDGE : 2 * KEYS + 2 * EDGE, :] = miss(halo[EDGE : 2 * EDGE, 512:640], before)
    for group in range(3):
        at = (group + 2) * EDGE
        region = halo[at : at + EDGE, 512:640].astype(F32)
        f_kb[group * KEYS + 2 * EDGE : (group + 1) * KEYS, :] = miss(
            jnp.where(column < 16, region, ends)
        )
    for ref, value in (
        (kb, keys_of(halo[:, 0:512], w_b)),
        (vb, values_of(halo[:, 0:512], w_b)),
    ):
        ref[0:EDGE, :] = value[0:EDGE]
        ref[2 * KEYS + EDGE : 2 * KEYS + 2 * EDGE, :] = value[EDGE : 2 * EDGE]
        for group in range(3):
            at = (group + 2) * EDGE
            ref[group * KEYS + 2 * EDGE : (group + 1) * KEYS, :] = value[at : at + EDGE]

    def pair_b(pair, carry):
        cut = lanes(pair)
        outs = []
        for group, (start, size) in enumerate(((0, EDGE), (64, 2 * EDGE), (TOK - EDGE, EDGE))):
            keys = slice(group * KEYS, (group + 1) * KEYS)
            out, _ = attend_pair(
                qa[start : start + size, cut],
                kb[keys, cut],
                vb[keys, cut],
                hid_t[start : start + size, 512:640],
                f_kb[keys, :],
            )
            outs.append(out)
        first, second, third = outs
        upper = lax.broadcasted_iota(jnp.int32, (16, FEAT), 0) < 8
        att[0:64, cut] = first[0:64].astype(BF)
        att[64:80, cut] = jnp.where(upper, first[64:80], second[0:16]).astype(BF)
        att[80:208, cut] = second[16:144].astype(BF)
        att[208:224, cut] = jnp.where(upper, second[144:160], third[0:16]).astype(BF)
        att[224:288, cut] = third[16:80].astype(BF)
        return carry

    lax.fori_loop(0, 4, pair_b, 0, unroll=True)


def attend_pair_back(q, k, v, grad, out, exps):
    dq = dk = dv = None
    right = wide(grad, grad * out)
    for mask, exp in zip(pair_masks(), exps):
        slope = dot_nt(wide(v * mask, -mask), right)
        d_scores = exp * slope.astype(BF)
        q_part = dot_tn(d_scores, k * mask)
        k_part = dot(d_scores, q * mask)
        v_part = dot(exp, grad * mask)
        dq = q_part if dq is None else dq + q_part
        dk = k_part if dk is None else dk + k_part
        dv = v_part if dv is None else dv + v_part
    return dq, dk, dv


def backward_kernel(
    att, hid_t, pred, o_s, rq_s, rk_s, rd_s, q_s, k_s, v_s, att_s, exps_s,
    tout_b, sqkv, sout, sproj, heads,
    out_ref, grad_ref,
    da_s, dq_s, dk_s, dv_s,
):
    o = dot(att[...], tout_b[...])
    result = (hid_t[:, 0:512].astype(F32) + o * normed(o)).astype(BF)
    out_ref[...] = result
    residual = pred[...] - result.astype(F32)
    g = dot_nt(residual.astype(BF), sproj[...]).astype(BF).astype(F32)
    for layer in (1, 0):
        o = o_s[layer]
        scale = normed(o)
        y = o * scale
        d_o = scale * (g - y * jnp.mean(g * y, axis=-1, keepdims=True))
        da = dot_nt(d_o.astype(BF), sout[layer]).astype(BF)
        da_s[...] = (da.astype(F32) * rd_s[layer]).astype(BF)
        for pair in range(2):
            cut = slice(pair * 128, pair * 128 + 128)
            for group in range(2):
                rows = rows_of(group)
                first = layer * 4 + pair * 2
                dq, dk, dv = attend_pair_back(
                    q_s[layer, rows, cut],
                    k_s[layer, rows, cut],
                    v_s[layer, rows, cut],
                    da_s[rows, cut],
                    att_s[layer, rows, cut],
                    (exps_s[first, rows, :], exps_s[first + 1, rows, :]),
                )
                dq_s[rows, cut] = dq
                dk_s[rows, cut] = dk
                dv_s[rows, cut] = dv.astype(BF)
        dq = dq_s[...] * SCALE
        q_hat = q_s[layer].astype(F32) * (1.0 / (SCALE * LOG2E))
        along = dot((q_hat * dq).astype(BF), heads[...])
        dq = (rq_s[layer] * (dq - q_hat * along)).astype(BF)
        dk = dk_s[...] * (1.0 / LOG2E)
        k_hat = k_s[layer].astype(F32)
        along = dot((k_hat * dk).astype(BF), heads[...])
        dk = (rk_s[layer] * (dk - k_hat * along)).astype(BF)
        w = sqkv.at[layer]
        g = g + (
            dot_nt(dq, w[:, 0:256])
            + dot_nt(dk, w[:, 256:512])
            + dot_nt(dv_s[...], w[:, 512:768])
        )
        if layer == 1:
            g = g.astype(BF).astype(F32)
    grad_ref[...] = g


def solution(mesh):
    n_lat, n_lon = mesh.shape["lat"], mesh.shape["lon"]

    def shards(teacher_in, student_in, regions, t_qkv, t_out, s_qkv, s_out, s_proj):
        assert teacher_in.shape == (1, ROWS, COLS, 512)
        vm = pl.BlockSpec(memory_space=pltpu.VMEM)
        hbm = pl.BlockSpec(memory_space=pltpu.HBM)
        state = [
            ((TOK, 512), BF),
            ((TOK, 640), BF),
            ((TOK, 512), F32),
            ((2, TOK, 256), F32),
            ((2, TOK, 256), F32),
            ((2, TOK, 256), F32),
            ((2, TOK, 256), F32),
            ((2, TOK, 256), BF),
            ((2, TOK, 256), BF),
            ((2, TOK, 256), BF),
            ((2, TOK, 256), BF),
            ((8, TOK, GROUP), BF),
            (t_out.shape[1:], BF),
            (s_qkv.shape, BF),
            (s_out.shape, BF),
            (s_proj.shape, BF),
            ((256, 256), BF),
        ]
        scratch = [
            ((TOK, 512), BF),
            ((TOK, 256), BF),
            ((COLS, 2, ROWS), jnp.int32),
            (t_qkv.shape, BF),
            (t_out.shape[1:], BF),
            ((PACK, TOK), BF),
            ((KEYS, PACK), BF),
            ((4 * TOK, FEAT), BF),
            ((128, 128), F32),
            ((TOK, 512), BF),
            ((TOK, 512), BF),
            ((2, TOK, 512), BF),
            ((2, TOK, 512), BF),
            ((TOK, FEAT), BF),
            ((2, TOK, FEAT), BF),
            ((TOK, 256), BF),
            ((PACK, 640), BF),
            ((PACK, 640), BF),
            ((HALO, 640), BF),
            ((3 * KEYS, 512), BF),
            ((3 * KEYS, 512), BF),
            ((3 * KEYS, FEAT), BF),
        ]

        def columns_first(block):
            return block[0].transpose(1, 0, 2).reshape(TOK, block.shape[-1])

        def rows_first(block):
            return block.reshape(COLS, ROWS, block.shape[-1]).transpose(1, 0, 2)[None]

        def shapes(entries):
            return tuple(jax.ShapeDtypeStruct(shape, kind) for shape, kind in entries)

        def buffers(entries):
            return [pltpu.VMEM(shape, kind) for shape, kind in entries]

        operands = (
            columns_first(teacher_in),
            columns_first(student_in),
            regions.transpose(2, 0, 1),
            t_qkv,
            t_out,
            s_qkv,
            s_out,
            s_proj,
        ) + constants()
        operands = tuple(
            pltpu.with_memory_space_constraint(operand, pltpu.HBM) for operand in operands
        )
        saved = pl.pallas_call(
            functools.partial(forward_kernel, n_lat, n_lon),
            out_shape=shapes(state),
            in_specs=[hbm] * len(operands),
            out_specs=(vm,) * len(state),
            scratch_shapes=buffers(scratch)
            + [pltpu.SemaphoreType.DMA((count,)) for count in (14, 9, 9)],
            compiler_params=pltpu.CompilerParams(
                collective_id=0, has_side_effects=True, vmem_limit_bytes=K1_VMEM
            ),
            name="forward",
        )(*operands)
        teacher_out, grad = pl.pallas_call(
            backward_kernel,
            out_shape=shapes((((TOK, 512), BF), ((TOK, 256), F32))),
            in_specs=[vm] * len(saved),
            out_specs=(vm, vm),
            scratch_shapes=buffers(
                (((TOK, 256), BF), ((TOK, 256), F32), ((TOK, 256), F32), ((TOK, 256), BF))
            ),
            compiler_params=pltpu.CompilerParams(vmem_limit_bytes=K2_VMEM),
            name="backward",
        )(*saved)
        return rows_first(teacher_out), rows_first(grad)

    return jax.shard_map(
        shards,
        mesh=mesh,
        in_specs=(
            P("grp", "lat", "lon", None),
            P("grp", "lat", "lon", None),
            P(None, "lat", "lon"),
            P(),
            P(),
            P(),
            P(),
            P(),
        ),
        out_specs=(P("grp", "lat", "lon", None), P("grp", "lat", "lon", None)),
        check_vma=False,
    )
```

```python
import functools

import jax
import jax.numpy as jnp
import numpy as np
from jax import lax
from jax.experimental import pallas as pl
from jax.experimental.pallas import tpu as pltpu
from jax.sharding import PartitionSpec as P

HEADS_T = 8
HEADS_S = 4
SCALE = 10.0
EPS = 1e-06
BF = jnp.bfloat16
F32 = jnp.float32
MESH = pl.DeviceIdType.MESH

ROWS, COLS = 24, 12
TOK = ROWS * COLS
GROUP = 6 * ROWS
EDGE = 80
KEYS = 3 * EDGE
HALO = 5 * EDGE
FEAT = 128
LOG2E = 1.4426950408889634
MISS = 512.0
SEC_T, SEC_B, SEC_TL, SEC_BL, SEC_TR, SEC_BR = (
    (0, 80),
    (80, 80),
    (160, 32),
    (192, 32),
    (224, 32),
    (256, 32),
)
PACK = 288
K1_VMEM = 32 * 1024 * 1024
K2_VMEM = 32 * 1024 * 1024
DEPTH_S, DEPTH_A, DEPTH_B, DEPTH_G = 3, 3, 3, 2


def dot(a, b):
    return jnp.dot(a, b, preferred_element_type=F32)


def dot_nt(a, b):
    return lax.dot_general(a, b, (((1,), (1,)), ((), ())), preferred_element_type=F32)


def dot_tn(a, b):
    return lax.dot_general(a, b, (((0,), (0,)), ((), ())), preferred_element_type=F32)


def constants():
    gather = np.zeros((PACK, TOK), np.float32)

    def put(section, cols, rows):
        at = section[0]
        for col in cols:
            for row in rows:
                gather[at, col * ROWS + row] = 1
                at += 1

    top, bottom = range(6), range(ROWS - 6, ROWS)
    first, last = range(3), range(COLS - 3, COLS)
    put(SEC_T, range(COLS), bottom)
    put(SEC_B, range(COLS), top)
    put(SEC_TL, last, bottom)
    put(SEC_BL, last, top)
    put(SEC_TR, first, bottom)
    put(SEC_BR, first, top)
    spread = np.zeros((3 * EDGE, PACK), np.float32)
    for group in range(3):
        for place in range(6):
            col = group * 6 + place - 3
            for end, (mid, before, after) in enumerate(
                ((SEC_T, SEC_TL, SEC_TR), (SEC_B, SEC_BL, SEC_BR))
            ):
                if col < 0:
                    source = before[0] + (col + 3) * 6
                elif col >= COLS:
                    source = after[0] + (col - COLS) * 6
                else:
                    source = mid[0] + col * 6
                for row in range(6):
                    spread[group * EDGE + end * 36 + place * 6 + row, source + row] = 1
    token = np.arange(TOK)[:, None]
    lane = np.arange(FEAT)[None, :]
    marks = np.concatenate(
        [
            token // ROWS == lane,
            token % ROWS == lane,
            16 + token % ROWS // 12 == lane,
            16 + (token % ROWS + 6) // 12 == lane,
        ]
    ).astype(np.float32)
    heads = (np.arange(256)[:, None] // 64 == np.arange(256)[None, :] // 64).astype(np.float32)
    return tuple(jnp.asarray(table, BF) for table in (gather, spread, marks, heads))


def inverse_norm(values, heads):
    square = (values * values).astype(BF)
    parts = [
        dot(square[:, at : at + 256], heads) for at in range(0, values.shape[1], 256)
    ]
    total = parts[0] if len(parts) == 1 else jnp.concatenate(parts, axis=1)
    return lax.rsqrt(total + EPS)


def pair_masks():
    lane = lax.broadcasted_iota(jnp.int32, (1, FEAT), 1)
    low = jnp.where(lane < 64, 1.0, 0.0).astype(F32)
    return low.astype(BF), (1.0 - low).astype(BF)


def wide(left, right):
    return jnp.concatenate([left, jnp.broadcast_to(right, left.shape)], axis=1)


def pipelined(jobs, depth=3):
    waiting = [start() for start, _ in jobs[:depth]]
    for at, (_, finish) in enumerate(jobs):
        scores = waiting.pop(0)
        if at + depth < len(jobs):
            waiting.append(jobs[at + depth][0]())
        finish(scores)


def masked(read, tile):
    masks = pair_masks()
    if tile < 2:
        return read(slice(0, 256), masks[tile])
    return jnp.concatenate([read(slice(256, None), mask) for mask in masks], axis=0)


def attend_jobs(q, k, v, f_query, f_key, done):
    total = []

    def scores(tile):
        def read(rows, mask):
            return wide(k(rows) * mask, f_key(rows))

        return dot_nt(wide(q(), f_query()), masked(read, tile))

    def gather(tile, last, values):
        def read(rows, mask):
            return wide(v(rows) * mask, mask)

        part = dot(jnp.exp2(values).astype(BF), masked(read, tile))
        total.append(part + total[-1] if total else part)
        if last:
            inverse = 1.0 / total[-1][:, FEAT:]
            done(total[-1][:, :FEAT] * inverse, inverse)

    tiles = 3 if k(slice(0, None)).shape[0] > 256 else 2
    return [
        (functools.partial(scores, tile), functools.partial(gather, tile, tile == tiles - 1))
        for tile in range(tiles)
    ]


def lanes(pair):
    return slice(pair * 128, pair * 128 + 128)


def rows_of(group):
    return slice(group * GROUP, (group + 1) * GROUP)


def normed(o):
    return lax.rsqrt(jnp.mean(o * o, axis=-1, keepdims=True) + EPS)


def forward_kernel(n_lat, n_lon, *refs):
    (
        x_hbm, s_hbm, reg_hbm, tqkv_hbm, tout_hbm, sqkv_hbm, sout_hbm, sproj_hbm,
        gather_hbm, spread_hbm, marks_hbm, heads_hbm,
        att, hid_t, pred, o_s, rq_s, rk_s, rd_s, q_s, k_s, v_s, att_s, exps_s,
        tout_b, sqkv, sout, sproj, heads,
        x_ref, s_ref, reg_ref, tqkv, tout_a, gather, spread, marks,
        reg_pad, x_far, qa, ka, va, f_qa, f_ka, hid, pack, edge_in, halo, kb, vb, f_kb,
        load, send, recv,
    ) = refs
    lat, lon, grp = lax.axis_index("lat"), lax.axis_index("lon"), lax.axis_index("grp")
    right, left = lax.rem(lon + 1, n_lon), lax.rem(lon + n_lon - 1, n_lon)
    has_up, has_down = lat > 0, lat < n_lat - 1
    barrier = pltpu.get_barrier_semaphore()

    def greet(device):
        pl.semaphore_signal(barrier, inc=1, device_id=device, device_id_type=MESH)

    greet((lat, lon, 1 - grp))
    greet((lat, left, grp))
    greet((lat, right, grp))

    @pl.when(has_up)
    def _():
        for column in (left, lon, right):
            greet((lat - 1, column, grp))

    @pl.when(has_down)
    def _():
        for column in (left, lon, right):
            greet((lat + 1, column, grp))

    moves = dict(
        x=(x_hbm, x_ref),
        heads=(heads_hbm, heads),
        qkv_a=(tqkv_hbm.at[0], tqkv.at[0]),
        reg=(reg_hbm, reg_ref),
        marks=(marks_hbm, marks),
        tout_a=(tout_hbm.at[0], tout_a),
        gather=(gather_hbm, gather),
        s=(s_hbm, s_ref),
        sqkv=(sqkv_hbm, sqkv),
        sout=(sout_hbm, sout),
        qkv_b=(tqkv_hbm.at[1], tqkv.at[1]),
        sproj=(sproj_hbm, sproj),
        spread=(spread_hbm, spread),
        tout_b=(tout_hbm.at[1], tout_b),
    )
    loads = {
        name: pltpu.make_async_copy(source, target, load.at[slot])
        for slot, (name, (source, target)) in enumerate(moves.items())
    }
    for copy in loads.values():
        copy.start()

    @pl.when(jnp.logical_not(has_up))
    def _():
        for at, size in (SEC_T, SEC_TL, SEC_TR):
            edge_in[at : at + size, :] = jnp.zeros((size, 640), BF)

    @pl.when(jnp.logical_not(has_down))
    def _():
        for at, size in (SEC_B, SEC_BL, SEC_BR):
            edge_in[at : at + size, :] = jnp.zeros((size, 640), BF)

    def student_forward(layer, source_ref):
        source = source_ref[...]
        w = sqkv.at[layer]
        q = dot(source, w[:, 0:256]).astype(BF).astype(F32)
        rq = inverse_norm(q, heads[...])
        rq_s[layer] = rq
        q_s[layer] = (q * (rq * (SCALE * LOG2E))).astype(BF)
        k = dot(source, w[:, 256:512]).astype(BF).astype(F32)
        rk = inverse_norm(k, heads[...])
        rk_s[layer] = rk
        k_s[layer] = (k * rk).astype(BF)
        v_s[layer] = dot(source, w[:, 512:768]).astype(BF)
        jobs = []
        for pair in range(2):
            for group in range(2):
                cut, rows = lanes(pair), rows_of(group)

                def done(out, inverse, rows=rows, cut=cut):
                    att_s[layer, rows, cut] = out.astype(BF)
                    rd_s[layer, rows, cut] = inverse

                jobs += attend_jobs(
                    lambda rows=rows, cut=cut: q_s[layer, rows, cut],
                    lambda at, rows=rows, cut=cut: k_s[layer, rows, cut][at],
                    lambda at, rows=rows, cut=cut: v_s[layer, rows, cut][at],
                    lambda rows=rows: f_qa[rows, :],
                    lambda at, group=group: f_ka[group, 0:GROUP, :][at],
                    done,
                )
        pipelined(jobs, DEPTH_S)
        o = dot(att_s[layer], sout[layer])
        o_s[layer] = o
        return (source.astype(F32) + o * normed(o)).astype(BF)

    def keep_exps(layer):
        for pair in range(2):
            cut = lanes(pair)
            for group in range(2):
                rows = rows_of(group)
                query = wide(q_s[layer, rows, cut], f_qa[rows, :])
                for half, mask in enumerate(pair_masks()):
                    keys = wide(k_s[layer, rows, cut] * mask, f_ka[group, 0:GROUP, :])
                    exps_s[layer * 4 + pair * 2 + half, rows, :] = jnp.exp2(
                        dot_nt(keys, query)
                    ).astype(BF)

    def copy_to(source, target, slot, device):
        return pltpu.make_async_remote_copy(
            src_ref=source,
            dst_ref=target,
            send_sem=send.at[slot],
            recv_sem=recv.at[slot],
            device_id=device,
            device_id_type=MESH,
        )

    def keys_of(value, weight):
        keys = dot(value, weight[:, 512:1024]).astype(BF).astype(F32)
        return (keys * inverse_norm(keys, heads[...])).astype(BF)

    def values_of(value, weight):
        return dot(value, weight[:, 1024:1536]).astype(BF)

    def queries_of(value, weight):
        q = dot(value, weight[:, 0:512]).astype(BF).astype(F32)
        return (q * (inverse_norm(q, heads[...]) * (SCALE * LOG2E))).astype(BF)

    loads["x"].wait()
    loads["heads"].wait()
    rows_near = has_up.astype(jnp.int32) + has_down.astype(jnp.int32)
    pl.semaphore_wait(barrier, 3 + 3 * rows_near)

    to_partner = copy_to(x_ref, x_far, 0, (lat, lon, 1 - grp))
    to_partner.start()

    loads["qkv_a"].wait()
    w_a = tqkv.at[0]
    qa[...] = queries_of(x_ref[...], w_a)

    def place_a(source, side):
        for ref, project in ((ka, keys_of), (va, values_of)):
            value = project(source[...], w_a)
            for group in range(2):
                ref[group, side * GROUP : (side + 1) * GROUP, :] = value[rows_of(group)]

    place_a(x_ref, 0)
    reg_pad[...] = jnp.zeros_like(reg_pad)
    loads["reg"].wait()
    loads["marks"].wait()
    lane = lax.broadcasted_iota(jnp.int32, (TOK, FEAT), 1).astype(F32)
    levels = (reg_ref[:, 0, :], reg_ref[:, 1, :])
    window_a = marks[2 * TOK : 3 * TOK, :]
    for side, (one, two) in enumerate((levels, levels[::-1])):
        reg_pad[0:COLS, 0:ROWS] = jnp.where(grp == 0, one, two).astype(F32)
        region = jnp.sum(
            dot(marks[0:TOK, :], reg_pad[...].astype(BF))
            * marks[TOK : 2 * TOK, :].astype(F32),
            axis=1,
            keepdims=True,
        )
        hot = jnp.where(region == lane, 1.0, 0.0).astype(BF)
        feature = hot + window_a
        for group in range(2):
            f_ka[group, side * GROUP : (side + 1) * GROUP, :] = (
                feature[rows_of(group)] - 1
            ) * MISS
        if side == 0:
            f_qa[...] = feature
            hid_t[:, 512:640] = hot + marks[3 * TOK : 4 * TOK, :]

    to_partner.wait()
    place_a(x_far, 1)

    jobs = []
    for group in range(2):
        rows = rows_of(group)
        for pair in range(4):
            cut = lanes(pair)

            def done(out, _, rows=rows, cut=cut):
                att[rows, cut] = out.astype(BF)

            jobs += attend_jobs(
                lambda rows=rows, cut=cut: qa[rows, cut],
                lambda at, group=group, cut=cut: ka[group, at, cut],
                lambda at, group=group, cut=cut: va[group, at, cut],
                lambda rows=rows: f_qa[rows, :],
                lambda at, group=group: f_ka[group, at, :],
                done,
            )
    pipelined(jobs, DEPTH_A)
    loads["tout_a"].wait()
    o = dot(att[...], tout_a[...])
    hid_t[:, 0:512] = (x_ref[...].astype(F32) + o * normed(o)).astype(BF)

    to_right = copy_to(hid_t.at[TOK - EDGE : TOK], halo.at[0:EDGE], 1, (lat, right, grp))
    to_left = copy_to(hid_t.at[0:EDGE], halo.at[EDGE : 2 * EDGE], 2, (lat, left, grp))
    to_right.start()
    to_left.start()
    loads["gather"].wait()
    pack[...] = dot(gather[...], hid_t[...]).astype(BF)

    def section(sec, slot, device):
        piece = pl.ds(sec[0], sec[1])
        return copy_to(pack.at[piece], edge_in.at[piece], slot, device)

    ups = (
        section(SEC_B, 3, (lat - 1, lon, grp)),
        section(SEC_BL, 4, (lat - 1, right, grp)),
        section(SEC_BR, 5, (lat - 1, left, grp)),
    )
    downs = (
        section(SEC_T, 6, (lat + 1, lon, grp)),
        section(SEC_TL, 7, (lat + 1, right, grp)),
        section(SEC_TR, 8, (lat + 1, left, grp)),
    )

    @pl.when(has_up)
    def _():
        for copy in ups:
            copy.start()

    @pl.when(has_down)
    def _():
        for copy in downs:
            copy.start()

    place = lax.broadcasted_iota(jnp.int32, (EDGE, FEAT), 0)
    after, before = place >= 8, place < EDGE - 8

    def miss(feature, keep=None):
        feature = feature.astype(F32)
        if keep is not None:
            feature = jnp.where(keep, feature, 0.0)
        return ((feature - 1.0) * MISS).astype(BF)

    own = hid_t[:, 512:640]
    f_kb[EDGE : 2 * EDGE, :] = miss(own[0:EDGE], before)
    f_kb[KEYS : KEYS + EDGE, :] = miss(own[64 : 64 + EDGE], after)
    f_kb[KEYS + EDGE : KEYS + 2 * EDGE, :] = miss(own[64 + EDGE : 64 + 2 * EDGE], before)
    f_kb[2 * KEYS : 2 * KEYS + EDGE, :] = miss(own[TOK - EDGE :], after)

    loads["qkv_b"].wait()
    w_b = tqkv.at[1]
    qa[...] = queries_of(hid_t[:, 0:512], w_b)
    for ref, value in (
        (kb, keys_of(hid_t[:, 0:512], w_b)),
        (vb, values_of(hid_t[:, 0:512], w_b)),
    ):
        ref[EDGE : 2 * EDGE, :] = value[0:EDGE]
        ref[KEYS : KEYS + 2 * EDGE, :] = value[64 : 64 + 2 * EDGE]
        ref[2 * KEYS : 2 * KEYS + EDGE, :] = value[TOK - EDGE :]

    for name in ("s", "sqkv", "sout"):
        loads[name].wait()
    hid[...] = student_forward(0, s_ref)

    keep_exps(0)
    last = student_forward(1, hid)
    loads["sproj"].wait()
    pred[...] = dot(last, sproj[...])
    keep_exps(1)
    loads["spread"].wait()
    loads["tout_b"].wait()

    to_right.wait()
    to_left.wait()

    @pl.when(has_up)
    def _():
        for copy in ups:
            copy.wait_send()
        for copy in downs:
            copy.wait_recv()

    @pl.when(has_down)
    def _():
        for copy in downs:
            copy.wait_send()
        for copy in ups:
            copy.wait_recv()

    halo[2 * EDGE :, :] = dot(spread[...], edge_in[...]).astype(BF)
    column = lax.broadcasted_iota(jnp.int32, (EDGE, FEAT), 1)
    window_b = jnp.where(place < 36, 16, jnp.where(place < 72, 18, FEAT))
    ends = jnp.where(column == window_b, 1.0, 0.0)
    f_kb[0:EDGE, :] = miss(halo[0:EDGE, 512:640], after)
    f_kb[2 * KEYS + EDGE : 2 * KEYS + 2 * EDGE, :] = miss(halo[EDGE : 2 * EDGE, 512:640], before)
    for group in range(3):
        at = (group + 2) * EDGE
        region = halo[at : at + EDGE, 512:640].astype(F32)
        f_kb[group * KEYS + 2 * EDGE : (group + 1) * KEYS, :] = miss(
            jnp.where(column < 16, region, ends)
        )
    for ref, value in (
        (kb, keys_of(halo[:, 0:512], w_b)),
        (vb, values_of(halo[:, 0:512], w_b)),
    ):
        ref[0:EDGE, :] = value[0:EDGE]
        ref[2 * KEYS + EDGE : 2 * KEYS + 2 * EDGE, :] = value[EDGE : 2 * EDGE]
        for group in range(3):
            at = (group + 2) * EDGE
            ref[group * KEYS + 2 * EDGE : (group + 1) * KEYS, :] = value[at : at + EDGE]

    jobs = []
    for pair in range(4):
        cut = lanes(pair)
        outs = []

        def done(out, _, outs=outs, cut=cut):
            outs.append(out)
            if len(outs) < 3:
                return
            first, second, third = outs
            upper = lax.broadcasted_iota(jnp.int32, (16, FEAT), 0) < 8
            att[0:64, cut] = first[0:64].astype(BF)
            att[64:80, cut] = jnp.where(upper, first[64:80], second[0:16]).astype(BF)
            att[80:208, cut] = second[16:144].astype(BF)
            att[208:224, cut] = jnp.where(upper, second[144:160], third[0:16]).astype(BF)
            att[224:288, cut] = third[16:80].astype(BF)

        for group, (start, size) in enumerate(((0, EDGE), (64, 2 * EDGE), (TOK - EDGE, EDGE))):
            rows = slice(start, start + size)
            keys = slice(group * KEYS, (group + 1) * KEYS)
            jobs += attend_jobs(
                lambda rows=rows, cut=cut: qa[rows, cut],
                lambda at, keys=keys, cut=cut: kb[keys, cut][at],
                lambda at, keys=keys, cut=cut: vb[keys, cut][at],
                lambda rows=rows: hid_t[rows, 512:640],
                lambda at, keys=keys: f_kb[keys, :][at],
                done,
            )
    pipelined(jobs, DEPTH_B)


def backward_kernel(
    att, hid_t, pred, o_s, rq_s, rk_s, rd_s, q_s, k_s, v_s, att_s, exps_s,
    tout_b, sqkv, sout, sproj, heads,
    out_ref, grad_ref,
    da_s, dq_s, dk_s, dv_s,
):
    o = dot(att[...], tout_b[...])
    result = (hid_t[:, 0:512].astype(F32) + o * normed(o)).astype(BF)
    out_ref[...] = result
    residual = pred[...] - result.astype(F32)
    g = dot_nt(residual.astype(BF), sproj[...]).astype(BF).astype(F32)
    for layer in (1, 0):
        o = o_s[layer]
        scale = normed(o)
        y = o * scale
        d_o = scale * (g - y * jnp.mean(g * y, axis=-1, keepdims=True))
        da = dot_nt(d_o.astype(BF), sout[layer]).astype(BF)
        da_s[...] = (da.astype(F32) * rd_s[layer]).astype(BF)
        jobs = []
        for pair in range(2):
            for group in range(2):
                cut, rows = lanes(pair), rows_of(group)
                sums = []
                for half, mask in enumerate(pair_masks()):

                    def slope(rows=rows, cut=cut, mask=mask):
                        grad = da_s[rows, cut]
                        return dot_nt(
                            wide(v_s[layer, rows, cut] * mask, -mask),
                            wide(grad, grad * att_s[layer, rows, cut]),
                        )

                    def spread(slopes, rows=rows, cut=cut, mask=mask, sums=sums, at=layer * 4 + pair * 2 + half):
                        exps = exps_s[at, rows, :]
                        d_scores = exps * slopes.astype(BF)
                        parts = (
                            dot_tn(d_scores, k_s[layer, rows, cut] * mask),
                            dot(d_scores, q_s[layer, rows, cut] * mask),
                            dot(exps, da_s[rows, cut] * mask),
                        )
                        if not sums:
                            sums.append(parts)
                            return
                        dq, dk, dv = (one + two for one, two in zip(sums[0], parts))
                        dq_s[rows, cut] = dq
                        dk_s[rows, cut] = dk
                        dv_s[rows, cut] = dv.astype(BF)

                    jobs.append((slope, spread))
        pipelined(jobs, DEPTH_G)
        dq = dq_s[...] * SCALE
        q_hat = q_s[layer].astype(F32) * (1.0 / (SCALE * LOG2E))
        along = dot((q_hat * dq).astype(BF), heads[...])
        dq = (rq_s[layer] * (dq - q_hat * along)).astype(BF)
        dk = dk_s[...] * (1.0 / LOG2E)
        k_hat = k_s[layer].astype(F32)
        along = dot((k_hat * dk).astype(BF), heads[...])
        dk = (rk_s[layer] * (dk - k_hat * along)).astype(BF)
        w = sqkv.at[layer]
        g = g + (
            dot_nt(dq, w[:, 0:256])
            + dot_nt(dk, w[:, 256:512])
            + dot_nt(dv_s[...], w[:, 512:768])
        )
        if layer == 1:
            g = g.astype(BF).astype(F32)
    grad_ref[...] = g


def solution(mesh):
    n_lat, n_lon = mesh.shape["lat"], mesh.shape["lon"]

    def shards(teacher_in, student_in, regions, t_qkv, t_out, s_qkv, s_out, s_proj):
        assert teacher_in.shape == (1, ROWS, COLS, 512)
        vm = pl.BlockSpec(memory_space=pltpu.VMEM)
        hbm = pl.BlockSpec(memory_space=pltpu.HBM)
        state = [
            ((TOK, 512), BF),
            ((TOK, 640), BF),
            ((TOK, 512), F32),
            ((2, TOK, 256), F32),
            ((2, TOK, 256), F32),
            ((2, TOK, 256), F32),
            ((2, TOK, 256), F32),
            ((2, TOK, 256), BF),
            ((2, TOK, 256), BF),
            ((2, TOK, 256), BF),
            ((2, TOK, 256), BF),
            ((8, TOK, GROUP), BF),
            (t_out.shape[1:], BF),
            (s_qkv.shape, BF),
            (s_out.shape, BF),
            (s_proj.shape, BF),
            ((256, 256), BF),
        ]
        scratch = [
            ((TOK, 512), BF),
            ((TOK, 256), BF),
            ((COLS, 2, ROWS), jnp.int32),
            (t_qkv.shape, BF),
            (t_out.shape[1:], BF),
            ((PACK, TOK), BF),
            ((KEYS, PACK), BF),
            ((4 * TOK, FEAT), BF),
            ((128, 128), F32),
            ((TOK, 512), BF),
            ((TOK, 512), BF),
            ((2, 2 * GROUP, 512), BF),
            ((2, 2 * GROUP, 512), BF),
            ((TOK, FEAT), BF),
            ((2, 2 * GROUP, FEAT), BF),
            ((TOK, 256), BF),
            ((PACK, 640), BF),
            ((PACK, 640), BF),
            ((HALO, 640), BF),
            ((3 * KEYS, 512), BF),
            ((3 * KEYS, 512), BF),
            ((3 * KEYS, FEAT), BF),
        ]

        def columns_first(block):
            return block[0].transpose(1, 0, 2).reshape(TOK, block.shape[-1])

        def rows_first(block):
            return block.reshape(COLS, ROWS, block.shape[-1]).transpose(1, 0, 2)[None]

        def shapes(entries):
            return tuple(jax.ShapeDtypeStruct(shape, kind) for shape, kind in entries)

        def buffers(entries):
            return [pltpu.VMEM(shape, kind) for shape, kind in entries]

        operands = (
            columns_first(teacher_in),
            columns_first(student_in),
            regions.transpose(2, 0, 1),
            t_qkv,
            t_out,
            s_qkv,
            s_out,
            s_proj,
        ) + constants()
        operands = tuple(
            pltpu.with_memory_space_constraint(operand, pltpu.HBM) for operand in operands
        )
        saved = pl.pallas_call(
            functools.partial(forward_kernel, n_lat, n_lon),
            out_shape=shapes(state),
            in_specs=[hbm] * len(operands),
            out_specs=(vm,) * len(state),
            scratch_shapes=buffers(scratch)
            + [pltpu.SemaphoreType.DMA((count,)) for count in (14, 9, 9)],
            compiler_params=pltpu.CompilerParams(
                collective_id=0, has_side_effects=True, vmem_limit_bytes=K1_VMEM
            ),
            name="forward",
        )(*operands)
        teacher_out, grad = pl.pallas_call(
            backward_kernel,
            out_shape=shapes((((TOK, 512), BF), ((TOK, 256), F32))),
            in_specs=[vm] * len(saved),
            out_specs=(vm, vm),
            scratch_shapes=buffers(
                (((TOK, 256), BF), ((TOK, 256), F32), ((TOK, 256), F32), ((TOK, 256), BF))
            ),
            compiler_params=pltpu.CompilerParams(vmem_limit_bytes=K2_VMEM),
            name="backward",
        )(*saved)
        return rows_first(teacher_out), rows_first(grad)

    return jax.shard_map(
        shards,
        mesh=mesh,
        in_specs=(
            P("grp", "lat", "lon", None),
            P("grp", "lat", "lon", None),
            P(None, "lat", "lon"),
            P(),
            P(),
            P(),
            P(),
            P(),
        ),
        out_specs=(P("grp", "lat", "lon", None), P("grp", "lat", "lon", None)),
        check_vma=False,
    )
```

```python
import functools

import jax
import jax.numpy as jnp
import numpy as np
from jax import lax
from jax.experimental import pallas as pl
from jax.experimental.pallas import tpu as pltpu
from jax.sharding import PartitionSpec as P

HEADS_T = 8
HEADS_S = 4
SCALE = 10.0
EPS = 1e-06
BF = jnp.bfloat16
F32 = jnp.float32
MESH = pl.DeviceIdType.MESH

ROWS, COLS = 24, 12
TOK = ROWS * COLS
GROUP = 6 * ROWS
EDGE = 80
KEYS = 3 * EDGE
HALO = 5 * EDGE
FEAT = 128
LOG2E = 1.4426950408889634
MISS = 512.0
SEC_T, SEC_B = ((0, 48), (160, 48)), ((48, 48), (208, 48))
SEC_TR, SEC_BR, SEC_TL, SEC_BL = (96, 32), (128, 32), (256, 32), (288, 32)
PACK = 320
PART = 160
K1_VMEM = 32 * 1024 * 1024
K2_VMEM = 32 * 1024 * 1024
DEPTH_S, DEPTH_A, DEPTH_B, DEPTH_G = 4, 4, 4, 4


def dot(a, b):
    return jnp.dot(a, b, preferred_element_type=F32)


def dot_nt(a, b):
    return lax.dot_general(a, b, (((1,), (1,)), ((), ())), preferred_element_type=F32)


def dot_tn(a, b):
    return lax.dot_general(a, b, (((0,), (0,)), ((), ())), preferred_element_type=F32)


def constants():
    gather = np.zeros((PACK, GROUP), np.float32)

    def put(section, cols, rows):
        at = section[0]
        for col in cols:
            for row in rows:
                gather[at, col % 6 * ROWS + row] = 1
                at += 1

    top, bottom = range(6), range(ROWS - 6, ROWS)
    first, last = range(3), range(COLS - 3, COLS)
    for half in range(2):
        put(SEC_T[half], range(6 * half, 6 * half + 6), bottom)
        put(SEC_B[half], range(6 * half, 6 * half + 6), top)
    put(SEC_TL, last, bottom)
    put(SEC_BL, last, top)
    put(SEC_TR, first, bottom)
    put(SEC_BR, first, top)
    spread = np.zeros((3 * EDGE, PACK), np.float32)
    for group in range(3):
        for place in range(6):
            col = group * 6 + place - 3
            for end, (mid, before, after) in enumerate(
                ((SEC_T, SEC_TL, SEC_TR), (SEC_B, SEC_BL, SEC_BR))
            ):
                if col < 0:
                    source = before[0] + (col + 3) * 6
                elif col >= COLS:
                    source = after[0] + (col - COLS) * 6
                else:
                    source = mid[col // 6][0] + col % 6 * 6
                for row in range(6):
                    spread[group * EDGE + end * 36 + place * 6 + row, source + row] = 1
    token = np.arange(TOK)[:, None]
    lane = np.arange(FEAT)[None, :]
    marks = np.concatenate(
        [
            token // ROWS == lane,
            token % ROWS == lane,
            16 + token % ROWS // 12 == lane,
            16 + (token % ROWS + 6) // 12 == lane,
        ]
    ).astype(np.float32)
    heads = (np.arange(256)[:, None] // 64 == np.arange(256)[None, :] // 64).astype(np.float32)
    return tuple(jnp.asarray(table, BF) for table in (gather, spread, marks, heads))


def inverse_norm(values, heads):
    square = (values * values).astype(BF)
    parts = [
        dot(square[:, at : at + 256], heads) for at in range(0, values.shape[1], 256)
    ]
    total = parts[0] if len(parts) == 1 else jnp.concatenate(parts, axis=1)
    return lax.rsqrt(total + EPS)


def pair_masks():
    lane = lax.broadcasted_iota(jnp.int32, (1, FEAT), 1)
    low = jnp.where(lane < 64, 1.0, 0.0).astype(F32)
    return low.astype(BF), (1.0 - low).astype(BF)


def wide(left, right):
    return jnp.concatenate([left, jnp.broadcast_to(right, left.shape)], axis=1)


def pipelined(jobs, depth=3):
    waiting = [start() for start, _ in jobs[:depth]]
    for at, (_, finish) in enumerate(jobs):
        scores = waiting.pop(0)
        if at + depth < len(jobs):
            waiting.append(jobs[at + depth][0]())
        finish(scores)


def masked(read, tile):
    masks = pair_masks()
    if tile < 2:
        return read(slice(0, 256), masks[tile])
    return jnp.concatenate([read(slice(256, None), mask) for mask in masks], axis=0)


def attend_jobs(q, k, v, f_query, f_key, done):
    total = []

    def scores(tile):
        def read(rows, mask):
            return wide(k(rows) * mask, f_key(rows))

        return dot_nt(wide(q(), f_query()), masked(read, tile))

    def gather(tile, last, values):
        def read(rows, mask):
            return wide(v(rows) * mask, mask)

        part = dot(jnp.exp2(values).astype(BF), masked(read, tile))
        total.append(part + total[-1] if total else part)
        if last:
            inverse = 1.0 / total[-1][:, FEAT:]
            done(total[-1][:, :FEAT] * inverse, inverse)

    tiles = 3 if k(slice(0, None)).shape[0] > 256 else 2
    return [
        (functools.partial(scores, tile), functools.partial(gather, tile, tile == tiles - 1))
        for tile in range(tiles)
    ]


def lanes(pair):
    return slice(pair * 128, pair * 128 + 128)


def rows_of(group):
    return slice(group * GROUP, (group + 1) * GROUP)


def normed(o):
    return lax.rsqrt(jnp.mean(o * o, axis=-1, keepdims=True) + EPS)


def forward_kernel(n_lat, n_lon, *refs):
    (
        x_hbm, s_hbm, reg_hbm, tqkv_hbm, tout_hbm, sqkv_hbm, sout_hbm, sproj_hbm,
        gather_hbm, spread_hbm, marks_hbm, heads_hbm,
        att, hid_t, pred, o_s, rq_s, rk_s, rd_s, q_s, k_s, v_s, att_s, exps_s,
        tout_b, sqkv, sout, sproj, heads,
        x_ref, s_ref, reg_ref, tqkv, tout_a, gather, spread, marks,
        reg_pad, x_far, qa, ka, va, f_qa, f_ka, hid, pack, edge_in, halo, kb, vb, f_kb,
        own_f, pack_f, edge_f, halo_f,
        load, send, recv,
    ) = refs
    lat, lon, grp = lax.axis_index("lat"), lax.axis_index("lon"), lax.axis_index("grp")
    right, left = lax.rem(lon + 1, n_lon), lax.rem(lon + n_lon - 1, n_lon)
    has_up, has_down = lat > 0, lat < n_lat - 1
    barrier = pltpu.get_barrier_semaphore()

    def greet(device):
        pl.semaphore_signal(barrier, inc=1, device_id=device, device_id_type=MESH)

    greet((lat, lon, 1 - grp))
    greet((lat, left, grp))
    greet((lat, right, grp))

    @pl.when(has_up)
    def _():
        for column in (left, lon, right):
            greet((lat - 1, column, grp))

    @pl.when(has_down)
    def _():
        for column in (left, lon, right):
            greet((lat + 1, column, grp))

    moves = dict(
        x=(x_hbm, x_ref),
        heads=(heads_hbm, heads),
        gather=(gather_hbm, gather),
        qkv_a=(tqkv_hbm.at[0], tqkv.at[0]),
        reg=(reg_hbm, reg_ref),
        marks=(marks_hbm, marks),
        tout_a=(tout_hbm.at[0], tout_a),
        s=(s_hbm, s_ref),
        sqkv=(sqkv_hbm, sqkv),
        sout=(sout_hbm, sout),
        qkv_b=(tqkv_hbm.at[1], tqkv.at[1]),
        sproj=(sproj_hbm, sproj),
        spread=(spread_hbm, spread),
        tout_b=(tout_hbm.at[1], tout_b),
    )
    loads = {
        name: pltpu.make_async_copy(source, target, load.at[slot])
        for slot, (name, (source, target)) in enumerate(moves.items())
    }
    for copy in loads.values():
        copy.start()

    def clear(sections):
        for at, size in sections:
            edge_in[at : at + size, :] = jnp.zeros((size, 512), BF)
            edge_f[at : at + size, :] = jnp.zeros((size, FEAT), BF)

    pl.when(jnp.logical_not(has_up))(lambda: clear((*SEC_T, SEC_TL, SEC_TR)))
    pl.when(jnp.logical_not(has_down))(lambda: clear((*SEC_B, SEC_BL, SEC_BR)))

    def student_forward(layer, source_ref):
        source = source_ref[...]
        w = sqkv.at[layer]
        q = dot(source, w[:, 0:256]).astype(BF).astype(F32)
        rq = inverse_norm(q, heads[...])
        rq_s[layer] = rq
        q_s[layer] = (q * (rq * (SCALE * LOG2E))).astype(BF)
        k = dot(source, w[:, 256:512]).astype(BF).astype(F32)
        rk = inverse_norm(k, heads[...])
        rk_s[layer] = rk
        k_s[layer] = (k * rk).astype(BF)
        v_s[layer] = dot(source, w[:, 512:768]).astype(BF)
        jobs = []
        for pair in range(2):
            for group in range(2):
                cut, rows = lanes(pair), rows_of(group)

                def done(out, inverse, rows=rows, cut=cut):
                    att_s[layer, rows, cut] = out.astype(BF)
                    rd_s[layer, rows, cut] = inverse

                jobs += attend_jobs(
                    lambda rows=rows, cut=cut: q_s[layer, rows, cut],
                    lambda at, rows=rows, cut=cut: k_s[layer, rows, cut][at],
                    lambda at, rows=rows, cut=cut: v_s[layer, rows, cut][at],
                    lambda rows=rows: f_qa[rows, :],
                    lambda at, group=group: f_ka[group, 0:GROUP, :][at],
                    done,
                )
        pipelined(jobs, DEPTH_S)
        o = dot(att_s[layer], sout[layer])
        o_s[layer] = o
        return (source.astype(F32) + o * normed(o)).astype(BF)

    def keep_exps(layer):
        for pair in range(2):
            cut = lanes(pair)
            for group in range(2):
                rows = rows_of(group)
                query = wide(q_s[layer, rows, cut], f_qa[rows, :])
                for half, mask in enumerate(pair_masks()):
                    keys = wide(k_s[layer, rows, cut] * mask, f_ka[group, 0:GROUP, :])
                    exps_s[layer * 4 + pair * 2 + half, rows, :] = jnp.exp2(
                        dot_nt(keys, query)
                    ).astype(BF)

    def copy_to(source, target, slot, device):
        return pltpu.make_async_remote_copy(
            src_ref=source,
            dst_ref=target,
            send_sem=send.at[slot],
            recv_sem=recv.at[slot],
            device_id=device,
            device_id_type=MESH,
        )

    def keys_of(value, weight):
        keys = dot(value, weight[:, 512:1024]).astype(BF).astype(F32)
        return (keys * inverse_norm(keys, heads[...])).astype(BF)

    def values_of(value, weight):
        return dot(value, weight[:, 1024:1536]).astype(BF)

    def queries_of(value, weight):
        q = dot(value, weight[:, 0:512]).astype(BF).astype(F32)
        return (q * (inverse_norm(q, heads[...]) * (SCALE * LOG2E))).astype(BF)

    w_a = tqkv.at[0]

    def place_a(source, side):
        for ref, project in ((ka, keys_of), (va, values_of)):
            value = project(source[...], w_a)
            for group in range(2):
                ref[group, side * GROUP : (side + 1) * GROUP, :] = value[rows_of(group)]

    def local_work():
        loads["qkv_a"].wait()
        qa[...] = queries_of(x_ref[...], w_a)
        place_a(x_ref, 0)
        reg_pad[...] = jnp.zeros_like(reg_pad)
        loads["reg"].wait()
        loads["marks"].wait()
        lane = lax.broadcasted_iota(jnp.int32, (TOK, FEAT), 1).astype(F32)
        levels = (reg_ref[:, 0, :], reg_ref[:, 1, :])
        window_a = marks[2 * TOK : 3 * TOK, :]
        for side, (one, two) in enumerate((levels, levels[::-1])):
            reg_pad[0:COLS, 0:ROWS] = jnp.where(grp == 0, one, two).astype(F32)
            region = jnp.sum(
                dot(marks[0:TOK, :], reg_pad[...].astype(BF))
                * marks[TOK : 2 * TOK, :].astype(F32),
                axis=1,
                keepdims=True,
            )
            hot = jnp.where(region == lane, 1.0, 0.0).astype(BF)
            feature = hot + window_a
            for group in range(2):
                f_ka[group, side * GROUP : (side + 1) * GROUP, :] = (
                    feature[rows_of(group)] - 1
                ) * MISS
            if side == 0:
                f_qa[...] = feature
                own_f[...] = hot + marks[3 * TOK : 4 * TOK, :]

    def student_work():
        for name in ("s", "sqkv", "sout"):
            loads[name].wait()
        hid[...] = student_forward(0, s_ref)

        keep_exps(0)
        last = student_forward(1, hid)
        loads["sproj"].wait()
        pred[...] = dot(last, sproj[...])
        keep_exps(1)

    loads["x"].wait()
    loads["heads"].wait()
    loads["gather"].wait()

    rows_near = has_up.astype(jnp.int32) + has_down.astype(jnp.int32)
    pl.semaphore_wait(barrier, 3 + 3 * rows_near)

    to_partner = copy_to(x_ref, x_far, 0, (lat, lon, 1 - grp))
    to_partner.start()

    local_work()

    def halves(slot, row, column, left, right, packed, edges, own, sides):
        def section(sec, at, device):
            piece = pl.ds(sec[0], sec[1])
            return copy_to(packed.at[piece], edges.at[piece], slot + at, device)

        def vertical(row, mids, before, after, at):
            return (
                (section(mids[0], at, (row, column, grp)), section(after, at + 1, (row, left, grp))),
                (section(mids[1], at + 2, (row, column, grp)), section(before, at + 3, (row, right, grp))),
            )

        ups = vertical(row - 1, SEC_B, SEC_BL, SEC_BR, 0)
        downs = vertical(row + 1, SEC_T, SEC_TL, SEC_TR, 4)
        along = (
            copy_to(own.at[0:EDGE], sides.at[EDGE : 2 * EDGE], slot + 8, (row, left, grp)),
            copy_to(own.at[TOK - EDGE : TOK], sides.at[0:EDGE], slot + 9, (row, right, grp)),
        )
        return ups, downs, along

    hidden_moves = halves(1, lat, lon, left, right, pack, edge_in, hid_t, halo)
    feature_moves = halves(11, lat, lon, left, right, pack_f, edge_f, own_f, halo_f)

    def start_half(moves, half):
        ups, downs, along = moves

        @pl.when(has_up)
        def _():
            for copy in ups[half]:
                copy.start()

        @pl.when(has_down)
        def _():
            for copy in downs[half]:
                copy.start()

    def wait_all(moves):
        ups, downs, along = moves
        for copy in along:
            copy.wait()

        @pl.when(has_up)
        def _():
            for copy in ups[0] + ups[1]:
                copy.wait_send()
            for copy in downs[0] + downs[1]:
                copy.wait_recv()

        @pl.when(has_down)
        def _():
            for copy in downs[0] + downs[1]:
                copy.wait_send()
            for copy in ups[0] + ups[1]:
                copy.wait_recv()

    for group in range(2):
        part = slice(group * PART, (group + 1) * PART)
        pack_f[part, :] = dot(gather[part, :], own_f[rows_of(group), :]).astype(BF)
    for group in range(2):
        feature_moves[2][group].start()
        start_half(feature_moves, group)

    to_partner.wait()
    place_a(x_far, 1)

    for group in range(2):
        jobs = []
        rows = rows_of(group)
        for pair in range(4):
            cut = lanes(pair)

            def done(out, _, rows=rows, cut=cut):
                att[rows, cut] = out.astype(BF)

            jobs += attend_jobs(
                lambda rows=rows, cut=cut: qa[rows, cut],
                lambda at, group=group, cut=cut: ka[group, at, cut],
                lambda at, group=group, cut=cut: va[group, at, cut],
                lambda rows=rows: f_qa[rows, :],
                lambda at, group=group: f_ka[group, at, :],
                done,
            )
        pipelined(jobs, DEPTH_A)
        if group == 0:
            loads["tout_a"].wait()
        o = dot(att[rows, :], tout_a[...])
        hid_t[rows, :] = (x_ref[rows, :].astype(F32) + o * normed(o)).astype(BF)
        hidden_moves[2][group].start()
        part = slice(group * PART, (group + 1) * PART)
        pack[part, :] = dot(gather[part, :], hid_t[rows, :]).astype(BF)
        start_half(hidden_moves, group)

    place = lax.broadcasted_iota(jnp.int32, (EDGE, FEAT), 0)
    after, before = place >= 8, place < EDGE - 8

    def miss(feature, keep=None):
        feature = feature.astype(F32)
        if keep is not None:
            feature = jnp.where(keep, feature, 0.0)
        return ((feature - 1.0) * MISS).astype(BF)

    own = own_f[...]
    f_kb[EDGE : 2 * EDGE, :] = miss(own[0:EDGE], before)
    f_kb[KEYS : KEYS + EDGE, :] = miss(own[64 : 64 + EDGE], after)
    f_kb[KEYS + EDGE : KEYS + 2 * EDGE, :] = miss(own[64 + EDGE : 64 + 2 * EDGE], before)
    f_kb[2 * KEYS : 2 * KEYS + EDGE, :] = miss(own[TOK - EDGE :], after)

    loads["qkv_b"].wait()
    w_b = tqkv.at[1]
    qa[...] = queries_of(hid_t[...], w_b)
    for ref, value in (
        (kb, keys_of(hid_t[...], w_b)),
        (vb, values_of(hid_t[...], w_b)),
    ):
        ref[EDGE : 2 * EDGE, :] = value[0:EDGE]
        ref[KEYS : KEYS + 2 * EDGE, :] = value[64 : 64 + 2 * EDGE]
        ref[2 * KEYS : 2 * KEYS + EDGE, :] = value[TOK - EDGE :]

    student_work()
    loads["spread"].wait()
    loads["tout_b"].wait()

    wait_all(feature_moves)
    edges_f = dot(spread[...], edge_f[...])
    column = lax.broadcasted_iota(jnp.int32, (EDGE, FEAT), 1)
    window_b = jnp.where(place < 36, 16, jnp.where(place < 72, 18, FEAT))
    ends = jnp.where(column == window_b, 1.0, 0.0)
    f_kb[0:EDGE, :] = miss(halo_f[0:EDGE, :], after)
    f_kb[2 * KEYS + EDGE : 2 * KEYS + 2 * EDGE, :] = miss(halo_f[EDGE : 2 * EDGE, :], before)
    for group in range(3):
        region = edges_f[group * EDGE : (group + 1) * EDGE]
        f_kb[group * KEYS + 2 * EDGE : (group + 1) * KEYS, :] = miss(
            jnp.where(column < 16, region, ends)
        )
    wait_all(hidden_moves)
    halo[2 * EDGE :, :] = dot(spread[...], edge_in[...]).astype(BF)
    for ref, value in (
        (kb, keys_of(halo[...], w_b)),
        (vb, values_of(halo[...], w_b)),
    ):
        ref[0:EDGE, :] = value[0:EDGE]
        ref[2 * KEYS + EDGE : 2 * KEYS + 2 * EDGE, :] = value[EDGE : 2 * EDGE]
        for group in range(3):
            at = (group + 2) * EDGE
            ref[group * KEYS + 2 * EDGE : (group + 1) * KEYS, :] = value[at : at + EDGE]

    jobs = []
    for pair in range(4):
        cut = lanes(pair)
        outs = []

        def done(out, _, outs=outs, cut=cut):
            outs.append(out)
            if len(outs) < 3:
                return
            first, second, third = outs
            upper = lax.broadcasted_iota(jnp.int32, (16, FEAT), 0) < 8
            att[0:64, cut] = first[0:64].astype(BF)
            att[64:80, cut] = jnp.where(upper, first[64:80], second[0:16]).astype(BF)
            att[80:208, cut] = second[16:144].astype(BF)
            att[208:224, cut] = jnp.where(upper, second[144:160], third[0:16]).astype(BF)
            att[224:288, cut] = third[16:80].astype(BF)

        for group, (start, size) in enumerate(((0, EDGE), (64, 2 * EDGE), (TOK - EDGE, EDGE))):
            rows = slice(start, start + size)
            keys = slice(group * KEYS, (group + 1) * KEYS)
            jobs += attend_jobs(
                lambda rows=rows, cut=cut: qa[rows, cut],
                lambda at, keys=keys, cut=cut: kb[keys, cut][at],
                lambda at, keys=keys, cut=cut: vb[keys, cut][at],
                lambda rows=rows: own_f[rows, :],
                lambda at, keys=keys: f_kb[keys, :][at],
                done,
            )
    pipelined(jobs, DEPTH_B)


def backward_kernel(
    att, hid_t, pred, o_s, rq_s, rk_s, rd_s, q_s, k_s, v_s, att_s, exps_s,
    tout_b, sqkv, sout, sproj, heads,
    out_ref, grad_ref,
    da_s, dq_s, dk_s, dv_s,
):
    o = dot(att[...], tout_b[...])
    result = (hid_t[:, 0:512].astype(F32) + o * normed(o)).astype(BF)
    out_ref[...] = result
    residual = pred[...] - result.astype(F32)
    g = dot_nt(residual.astype(BF), sproj[...]).astype(BF).astype(F32)
    for layer in (1, 0):
        o = o_s[layer]
        scale = normed(o)
        y = o * scale
        d_o = scale * (g - y * jnp.mean(g * y, axis=-1, keepdims=True))
        da = dot_nt(d_o.astype(BF), sout[layer]).astype(BF)
        da_s[...] = (da.astype(F32) * rd_s[layer]).astype(BF)
        jobs = []
        for pair in range(2):
            for group in range(2):
                cut, rows = lanes(pair), rows_of(group)
                sums = []
                for half, mask in enumerate(pair_masks()):

                    def slope(rows=rows, cut=cut, mask=mask):
                        grad = da_s[rows, cut]
                        return dot_nt(
                            wide(v_s[layer, rows, cut] * mask, -mask),
                            wide(grad, grad * att_s[layer, rows, cut]),
                        )

                    def spread(slopes, rows=rows, cut=cut, mask=mask, sums=sums, at=layer * 4 + pair * 2 + half):
                        exps = exps_s[at, rows, :]
                        d_scores = exps * slopes.astype(BF)
                        parts = (
                            dot_tn(d_scores, k_s[layer, rows, cut] * mask),
                            dot(d_scores, q_s[layer, rows, cut] * mask),
                            dot(exps, da_s[rows, cut] * mask),
                        )
                        if not sums:
                            sums.append(parts)
                            return
                        dq, dk, dv = (one + two for one, two in zip(sums[0], parts))
                        dq_s[rows, cut] = dq
                        dk_s[rows, cut] = dk
                        dv_s[rows, cut] = dv.astype(BF)

                    jobs.append((slope, spread))
        pipelined(jobs, DEPTH_G)
        dq = dq_s[...] * SCALE
        q_hat = q_s[layer].astype(F32) * (1.0 / (SCALE * LOG2E))
        along = dot((q_hat * dq).astype(BF), heads[...])
        dq = (rq_s[layer] * (dq - q_hat * along)).astype(BF)
        dk = dk_s[...] * (1.0 / LOG2E)
        k_hat = k_s[layer].astype(F32)
        along = dot((k_hat * dk).astype(BF), heads[...])
        dk = (rk_s[layer] * (dk - k_hat * along)).astype(BF)
        w = sqkv.at[layer]
        g = g + (
            dot_nt(dq, w[:, 0:256])
            + dot_nt(dk, w[:, 256:512])
            + dot_nt(dv_s[...], w[:, 512:768])
        )
        if layer == 1:
            g = g.astype(BF).astype(F32)
    grad_ref[...] = g


def solution(mesh):
    n_lat, n_lon = mesh.shape["lat"], mesh.shape["lon"]

    def shards(teacher_in, student_in, regions, t_qkv, t_out, s_qkv, s_out, s_proj):
        assert teacher_in.shape == (1, ROWS, COLS, 512)
        vm = pl.BlockSpec(memory_space=pltpu.VMEM)
        hbm = pl.BlockSpec(memory_space=pltpu.HBM)
        state = [
            ((TOK, 512), BF),
            ((TOK, 512), BF),
            ((TOK, 512), F32),
            ((2, TOK, 256), F32),
            ((2, TOK, 256), F32),
            ((2, TOK, 256), F32),
            ((2, TOK, 256), F32),
            ((2, TOK, 256), BF),
            ((2, TOK, 256), BF),
            ((2, TOK, 256), BF),
            ((2, TOK, 256), BF),
            ((8, TOK, GROUP), BF),
            (t_out.shape[1:], BF),
            (s_qkv.shape, BF),
            (s_out.shape, BF),
            (s_proj.shape, BF),
            ((256, 256), BF),
        ]
        scratch = [
            ((TOK, 512), BF),
            ((TOK, 256), BF),
            ((COLS, 2, ROWS), jnp.int32),
            (t_qkv.shape, BF),
            (t_out.shape[1:], BF),
            ((PACK, GROUP), BF),
            ((KEYS, PACK), BF),
            ((4 * TOK, FEAT), BF),
            ((128, 128), F32),
            ((TOK, 512), BF),
            ((TOK, 512), BF),
            ((2, 2 * GROUP, 512), BF),
            ((2, 2 * GROUP, 512), BF),
            ((TOK, FEAT), BF),
            ((2, 2 * GROUP, FEAT), BF),
            ((TOK, 256), BF),
            ((PACK, 512), BF),
            ((PACK, 512), BF),
            ((HALO, 512), BF),
            ((3 * KEYS, 512), BF),
            ((3 * KEYS, 512), BF),
            ((3 * KEYS, FEAT), BF),
            ((TOK, FEAT), BF),
            ((PACK, FEAT), BF),
            ((PACK, FEAT), BF),
            ((2 * EDGE, FEAT), BF),
        ]

        def columns_first(block):
            return block[0].transpose(1, 0, 2).reshape(TOK, block.shape[-1])

        def rows_first(block):
            return block.reshape(COLS, ROWS, block.shape[-1]).transpose(1, 0, 2)[None]

        def shapes(entries):
            return tuple(jax.ShapeDtypeStruct(shape, kind) for shape, kind in entries)

        def buffers(entries):
            return [pltpu.VMEM(shape, kind) for shape, kind in entries]

        operands = (
            columns_first(teacher_in),
            columns_first(student_in),
            regions.transpose(2, 0, 1),
            t_qkv,
            t_out,
            s_qkv,
            s_out,
            s_proj,
        ) + constants()
        operands = tuple(
            pltpu.with_memory_space_constraint(operand, pltpu.HBM) for operand in operands
        )
        saved = pl.pallas_call(
            functools.partial(forward_kernel, n_lat, n_lon),
            out_shape=shapes(state),
            in_specs=[hbm] * len(operands),
            out_specs=(vm,) * len(state),
            scratch_shapes=buffers(scratch)
            + [pltpu.SemaphoreType.DMA((count,)) for count in (14, 21, 21)],
            compiler_params=pltpu.CompilerParams(
                collective_id=0, has_side_effects=True, vmem_limit_bytes=K1_VMEM
            ),
            name="forward",
        )(*operands)
        teacher_out, grad = pl.pallas_call(
            backward_kernel,
            out_shape=shapes((((TOK, 512), BF), ((TOK, 256), F32))),
            in_specs=[vm] * len(saved),
            out_specs=(vm, vm),
            scratch_shapes=buffers(
                (((TOK, 256), BF), ((TOK, 256), F32), ((TOK, 256), F32), ((TOK, 256), BF))
            ),
            compiler_params=pltpu.CompilerParams(vmem_limit_bytes=K2_VMEM),
            name="backward",
        )(*saved)
        return rows_first(teacher_out), rows_first(grad)

    return jax.shard_map(
        shards,
        mesh=mesh,
        in_specs=(
            P("grp", "lat", "lon", None),
            P("grp", "lat", "lon", None),
            P(None, "lat", "lon"),
            P(),
            P(),
            P(),
            P(),
            P(),
        ),
        out_specs=(P("grp", "lat", "lon", None), P("grp", "lat", "lon", None)),
        check_vma=False,
    )
```

```python
import functools

import jax
import jax.numpy as jnp
import numpy as np
from jax import lax
from jax.experimental import pallas as pl
from jax.experimental.pallas import tpu as pltpu
from jax.sharding import PartitionSpec as P

HEADS_T = 8
HEADS_S = 4
SCALE = 10.0
EPS = 1e-06
BF = jnp.bfloat16
F32 = jnp.float32
MESH = pl.DeviceIdType.MESH

ROWS, COLS = 24, 12
TOK = ROWS * COLS
GROUP = 6 * ROWS
EDGE = 80
KEYS = 3 * EDGE
HALO = 5 * EDGE
FEAT = 128
LOG2E = 1.4426950408889634
MISS = 512.0
SEC_T, SEC_B = ((0, 48), (160, 48)), ((48, 48), (208, 48))
SEC_TR, SEC_BR, SEC_TL, SEC_BL = (96, 32), (128, 32), (256, 32), (288, 32)
PACK = 320
PART = 160
K1_VMEM = 32 * 1024 * 1024
K2_VMEM = 32 * 1024 * 1024
DEPTH_S, DEPTH_A, DEPTH_B, DEPTH_G = 4, 4, 4, 4


def dot(a, b):
    return jnp.dot(a, b, preferred_element_type=F32)


def dot_nt(a, b):
    return lax.dot_general(a, b, (((1,), (1,)), ((), ())), preferred_element_type=F32)


def dot_tn(a, b):
    return lax.dot_general(a, b, (((0,), (0,)), ((), ())), preferred_element_type=F32)


def constants():
    gather = np.zeros((PACK, GROUP), np.float32)

    def put(section, cols, rows):
        at = section[0]
        for col in cols:
            for row in rows:
                gather[at, col % 6 * ROWS + row] = 1
                at += 1

    top, bottom = range(6), range(ROWS - 6, ROWS)
    first, last = range(3), range(COLS - 3, COLS)
    for half in range(2):
        put(SEC_T[half], range(6 * half, 6 * half + 6), bottom)
        put(SEC_B[half], range(6 * half, 6 * half + 6), top)
    put(SEC_TL, last, bottom)
    put(SEC_BL, last, top)
    put(SEC_TR, first, bottom)
    put(SEC_BR, first, top)
    spread = np.zeros((3 * EDGE, PACK), np.float32)
    for group in range(3):
        for place in range(6):
            col = group * 6 + place - 3
            for end, (mid, before, after) in enumerate(
                ((SEC_T, SEC_TL, SEC_TR), (SEC_B, SEC_BL, SEC_BR))
            ):
                if col < 0:
                    source = before[0] + (col + 3) * 6
                elif col >= COLS:
                    source = after[0] + (col - COLS) * 6
                else:
                    source = mid[col // 6][0] + col % 6 * 6
                for row in range(6):
                    spread[group * EDGE + end * 36 + place * 6 + row, source + row] = 1
    token = np.arange(TOK)[:, None]
    lane = np.arange(FEAT)[None, :]
    marks = np.concatenate(
        [
            token // ROWS == lane,
            token % ROWS == lane,
            16 + token % ROWS // 12 == lane,
            16 + (token % ROWS + 6) // 12 == lane,
        ]
    ).astype(np.float32)
    heads = (np.arange(256)[:, None] // 64 == np.arange(256)[None, :] // 64).astype(np.float32)
    return tuple(jnp.asarray(table, BF) for table in (gather, spread, marks, heads))


def inverse_norm(values, heads):
    square = (values * values).astype(BF)
    parts = [
        dot(square[:, at : at + 256], heads) for at in range(0, values.shape[1], 256)
    ]
    total = parts[0] if len(parts) == 1 else jnp.concatenate(parts, axis=1)
    return lax.rsqrt(total + EPS)


def pair_masks():
    lane = lax.broadcasted_iota(jnp.int32, (1, FEAT), 1)
    low = jnp.where(lane < 64, 1.0, 0.0).astype(F32)
    return low.astype(BF), (1.0 - low).astype(BF)


def wide(left, right):
    return jnp.concatenate([left, jnp.broadcast_to(right, left.shape)], axis=1)


def pipelined(jobs, depth=3):
    waiting = [start() for start, _ in jobs[:depth]]
    for at, (_, finish) in enumerate(jobs):
        scores = waiting.pop(0)
        if at + depth < len(jobs):
            waiting.append(jobs[at + depth][0]())
        finish(scores)


def masked(read, tile):
    masks = pair_masks()
    if tile < 2:
        return read(slice(0, 256), masks[tile])
    return jnp.concatenate([read(slice(256, None), mask) for mask in masks], axis=0)


def attend_jobs(q, k, v, f_query, f_key, done, begin=None, whole=True):
    total = []

    def scores(tile):
        def read(rows, mask):
            return wide(k(rows) * mask, f_key(rows))

        return dot_nt(wide(q(), f_query()), masked(read, tile))

    def gather(tile, last, values):
        def read(rows, mask):
            return wide(v(rows) * mask, mask)

        part = dot(jnp.exp2(values).astype(BF), masked(read, tile))
        if total:
            part = part + total[-1]
        elif begin is not None:
            part = part + begin()
        total.append(part)
        if last and not whole:
            done(part)
        elif last:
            inverse = 1.0 / total[-1][:, FEAT:]
            done(total[-1][:, :FEAT] * inverse, inverse)

    tiles = 3 if k(slice(0, None)).shape[0] > 256 else 2
    return [
        (functools.partial(scores, tile), functools.partial(gather, tile, tile == tiles - 1))
        for tile in range(tiles)
    ]


def lanes(pair):
    return slice(pair * 128, pair * 128 + 128)


def rows_of(group):
    return slice(group * GROUP, (group + 1) * GROUP)


def normed(o):
    return lax.rsqrt(jnp.mean(o * o, axis=-1, keepdims=True) + EPS)


def forward_kernel(n_lat, n_lon, *refs):
    (
        x_hbm, s_hbm, reg_hbm, tqkv_hbm, tout_hbm, sqkv_hbm, sout_hbm, sproj_hbm,
        gather_hbm, spread_hbm, marks_hbm, heads_hbm,
        att, hid_t, pred, o_s, rq_s, rk_s, rd_s, q_s, k_s, v_s, att_s, exps_s,
        tout_b, sqkv, sout, sproj, heads,
        x_ref, s_ref, reg_ref, tqkv, tout_a, gather, spread, marks,
        reg_pad, x_far, qa, ka, va, f_qa, f_ka, hid, pack, edge_in, halo, kb, vb, f_kb,
        own_f, pack_f, edge_f, halo_f, near_b,
        load, send, recv,
    ) = refs
    lat, lon, grp = lax.axis_index("lat"), lax.axis_index("lon"), lax.axis_index("grp")
    right, left = lax.rem(lon + 1, n_lon), lax.rem(lon + n_lon - 1, n_lon)
    has_up, has_down = lat > 0, lat < n_lat - 1
    barrier = pltpu.get_barrier_semaphore()

    def greet(device):
        pl.semaphore_signal(barrier, inc=1, device_id=device, device_id_type=MESH)

    greet((lat, lon, 1 - grp))
    greet((lat, left, grp))
    greet((lat, right, grp))

    @pl.when(has_up)
    def _():
        for column in (left, lon, right):
            greet((lat - 1, column, grp))

    @pl.when(has_down)
    def _():
        for column in (left, lon, right):
            greet((lat + 1, column, grp))

    moves = dict(
        x=(x_hbm, x_ref),
        heads=(heads_hbm, heads),
        gather=(gather_hbm, gather),
        qkv_a=(tqkv_hbm.at[0], tqkv.at[0]),
        reg=(reg_hbm, reg_ref),
        marks=(marks_hbm, marks),
        tout_a=(tout_hbm.at[0], tout_a),
        s=(s_hbm, s_ref),
        sqkv=(sqkv_hbm, sqkv),
        sout=(sout_hbm, sout),
        qkv_b=(tqkv_hbm.at[1], tqkv.at[1]),
        sproj=(sproj_hbm, sproj),
        spread=(spread_hbm, spread),
        tout_b=(tout_hbm.at[1], tout_b),
    )
    loads = {
        name: pltpu.make_async_copy(source, target, load.at[slot])
        for slot, (name, (source, target)) in enumerate(moves.items())
    }
    for copy in loads.values():
        copy.start()

    def clear(sections):
        for at, size in sections:
            edge_in[at : at + size, :] = jnp.zeros((size, 512), BF)
            edge_f[at : at + size, :] = jnp.zeros((size, FEAT), BF)

    pl.when(jnp.logical_not(has_up))(lambda: clear((*SEC_T, SEC_TL, SEC_TR)))
    pl.when(jnp.logical_not(has_down))(lambda: clear((*SEC_B, SEC_BL, SEC_BR)))

    def student_forward(layer, source_ref):
        source = source_ref[...]
        w = sqkv.at[layer]
        q = dot(source, w[:, 0:256]).astype(BF).astype(F32)
        rq = inverse_norm(q, heads[...])
        rq_s[layer] = rq
        q_s[layer] = (q * (rq * (SCALE * LOG2E))).astype(BF)
        k = dot(source, w[:, 256:512]).astype(BF).astype(F32)
        rk = inverse_norm(k, heads[...])
        rk_s[layer] = rk
        k_s[layer] = (k * rk).astype(BF)
        v_s[layer] = dot(source, w[:, 512:768]).astype(BF)
        jobs = []
        for pair in range(2):
            for group in range(2):
                cut, rows = lanes(pair), rows_of(group)

                def done(out, inverse, rows=rows, cut=cut):
                    att_s[layer, rows, cut] = out.astype(BF)
                    rd_s[layer, rows, cut] = inverse

                jobs += attend_jobs(
                    lambda rows=rows, cut=cut: q_s[layer, rows, cut],
                    lambda at, rows=rows, cut=cut: k_s[layer, rows, cut][at],
                    lambda at, rows=rows, cut=cut: v_s[layer, rows, cut][at],
                    lambda rows=rows: f_qa[rows, :],
                    lambda at, group=group: f_ka[group, 0:GROUP, :][at],
                    done,
                )
        pipelined(jobs, DEPTH_S)
        o = dot(att_s[layer], sout[layer])
        o_s[layer] = o
        return (source.astype(F32) + o * normed(o)).astype(BF)

    def keep_exps(layer):
        for pair in range(2):
            cut = lanes(pair)
            for group in range(2):
                rows = rows_of(group)
                query = wide(q_s[layer, rows, cut], f_qa[rows, :])
                for half, mask in enumerate(pair_masks()):
                    keys = wide(k_s[layer, rows, cut] * mask, f_ka[group, 0:GROUP, :])
                    exps_s[layer * 4 + pair * 2 + half, rows, :] = jnp.exp2(
                        dot_nt(keys, query)
                    ).astype(BF)

    def copy_to(source, target, slot, device):
        return pltpu.make_async_remote_copy(
            src_ref=source,
            dst_ref=target,
            send_sem=send.at[slot],
            recv_sem=recv.at[slot],
            device_id=device,
            device_id_type=MESH,
        )

    def keys_of(value, weight):
        keys = dot(value, weight[:, 512:1024]).astype(BF).astype(F32)
        return (keys * inverse_norm(keys, heads[...])).astype(BF)

    def values_of(value, weight):
        return dot(value, weight[:, 1024:1536]).astype(BF)

    def queries_of(value, weight):
        q = dot(value, weight[:, 0:512]).astype(BF).astype(F32)
        return (q * (inverse_norm(q, heads[...]) * (SCALE * LOG2E))).astype(BF)

    w_a = tqkv.at[0]

    def place_a(source, side):
        for ref, project in ((ka, keys_of), (va, values_of)):
            value = project(source[...], w_a)
            for group in range(2):
                ref[group, side * GROUP : (side + 1) * GROUP, :] = value[rows_of(group)]

    def local_work():
        loads["qkv_a"].wait()
        qa[...] = queries_of(x_ref[...], w_a)
        place_a(x_ref, 0)
        reg_pad[...] = jnp.zeros_like(reg_pad)
        loads["reg"].wait()
        loads["marks"].wait()
        lane = lax.broadcasted_iota(jnp.int32, (TOK, FEAT), 1).astype(F32)
        levels = (reg_ref[:, 0, :], reg_ref[:, 1, :])
        window_a = marks[2 * TOK : 3 * TOK, :]
        for side, (one, two) in enumerate((levels, levels[::-1])):
            reg_pad[0:COLS, 0:ROWS] = jnp.where(grp == 0, one, two).astype(F32)
            region = jnp.sum(
                dot(marks[0:TOK, :], reg_pad[...].astype(BF))
                * marks[TOK : 2 * TOK, :].astype(F32),
                axis=1,
                keepdims=True,
            )
            hot = jnp.where(region == lane, 1.0, 0.0).astype(BF)
            feature = hot + window_a
            for group in range(2):
                f_ka[group, side * GROUP : (side + 1) * GROUP, :] = (
                    feature[rows_of(group)] - 1
                ) * MISS
            if side == 0:
                f_qa[...] = feature
                own_f[...] = hot + marks[3 * TOK : 4 * TOK, :]

    def student_work():
        for name in ("s", "sqkv", "sout"):
            loads[name].wait()
        hid[...] = student_forward(0, s_ref)

        keep_exps(0)
        last = student_forward(1, hid)
        loads["sproj"].wait()
        pred[...] = dot(last, sproj[...])
        keep_exps(1)

    loads["x"].wait()
    loads["heads"].wait()
    loads["gather"].wait()

    rows_near = has_up.astype(jnp.int32) + has_down.astype(jnp.int32)
    pl.semaphore_wait(barrier, 3 + 3 * rows_near)

    to_partner = copy_to(x_ref, x_far, 0, (lat, lon, 1 - grp))
    to_partner.start()

    local_work()

    def halves(slot, row, column, left, right, packed, edges, own, sides):
        def section(sec, at, device):
            piece = pl.ds(sec[0], sec[1])
            return copy_to(packed.at[piece], edges.at[piece], slot + at, device)

        def vertical(row, mids, before, after, at):
            return (
                (section(mids[0], at, (row, column, grp)), section(after, at + 1, (row, left, grp))),
                (section(mids[1], at + 2, (row, column, grp)), section(before, at + 3, (row, right, grp))),
            )

        ups = vertical(row - 1, SEC_B, SEC_BL, SEC_BR, 0)
        downs = vertical(row + 1, SEC_T, SEC_TL, SEC_TR, 4)
        along = (
            copy_to(own.at[0:EDGE], sides.at[EDGE : 2 * EDGE], slot + 8, (row, left, grp)),
            copy_to(own.at[TOK - EDGE : TOK], sides.at[0:EDGE], slot + 9, (row, right, grp)),
        )
        return ups, downs, along

    hidden_moves = halves(1, lat, lon, left, right, pack, edge_in, hid_t, halo)
    feature_moves = halves(11, lat, lon, left, right, pack_f, edge_f, own_f, halo_f)

    def start_half(moves, half):
        ups, downs, along = moves

        @pl.when(has_up)
        def _():
            for copy in ups[half]:
                copy.start()

        @pl.when(has_down)
        def _():
            for copy in downs[half]:
                copy.start()

    def wait_all(moves):
        ups, downs, along = moves
        for copy in along:
            copy.wait()

        @pl.when(has_up)
        def _():
            for copy in ups[0] + ups[1]:
                copy.wait_send()
            for copy in downs[0] + downs[1]:
                copy.wait_recv()

        @pl.when(has_down)
        def _():
            for copy in downs[0] + downs[1]:
                copy.wait_send()
            for copy in ups[0] + ups[1]:
                copy.wait_recv()

    for group in range(2):
        part = slice(group * PART, (group + 1) * PART)
        pack_f[part, :] = dot(gather[part, :], own_f[rows_of(group), :]).astype(BF)
    for group in range(2):
        feature_moves[2][group].start()
        start_half(feature_moves, group)

    to_partner.wait()
    place_a(x_far, 1)

    for group in range(2):
        jobs = []
        rows = rows_of(group)
        for pair in range(4):
            cut = lanes(pair)

            def done(out, _, rows=rows, cut=cut):
                att[rows, cut] = out.astype(BF)

            jobs += attend_jobs(
                lambda rows=rows, cut=cut: qa[rows, cut],
                lambda at, group=group, cut=cut: ka[group, at, cut],
                lambda at, group=group, cut=cut: va[group, at, cut],
                lambda rows=rows: f_qa[rows, :],
                lambda at, group=group: f_ka[group, at, :],
                done,
            )
        pipelined(jobs, DEPTH_A)
        if group == 0:
            loads["tout_a"].wait()
        o = dot(att[rows, :], tout_a[...])
        hid_t[rows, :] = (x_ref[rows, :].astype(F32) + o * normed(o)).astype(BF)
        hidden_moves[2][group].start()
        part = slice(group * PART, (group + 1) * PART)
        pack[part, :] = dot(gather[part, :], hid_t[rows, :]).astype(BF)
        start_half(hidden_moves, group)

    place = lax.broadcasted_iota(jnp.int32, (EDGE, FEAT), 0)
    after, before = place >= 8, place < EDGE - 8

    def miss(feature, keep=None):
        feature = feature.astype(F32)
        if keep is not None:
            feature = jnp.where(keep, feature, 0.0)
        return ((feature - 1.0) * MISS).astype(BF)

    own = own_f[...]
    f_kb[0:EDGE, :] = miss(own[0:EDGE], before)
    f_kb[KEYS : KEYS + EDGE, :] = miss(own[64 : 64 + EDGE], after)
    f_kb[KEYS + EDGE : KEYS + 2 * EDGE, :] = miss(own[64 + EDGE : 64 + 2 * EDGE], before)
    f_kb[2 * KEYS : 2 * KEYS + EDGE, :] = miss(own[TOK - EDGE :], after)

    loads["qkv_b"].wait()
    w_b = tqkv.at[1]
    qa[...] = queries_of(hid_t[...], w_b)
    for ref, value in (
        (kb, keys_of(hid_t[...], w_b)),
        (vb, values_of(hid_t[...], w_b)),
    ):
        ref[0:EDGE, :] = value[0:EDGE]
        ref[KEYS : KEYS + 2 * EDGE, :] = value[64 : 64 + 2 * EDGE]
        ref[2 * KEYS : 2 * KEYS + EDGE, :] = value[TOK - EDGE :]

    student_work()
    spans = ((0, EDGE, 0, EDGE), (64, 2 * EDGE, EDGE, 2 * EDGE), (TOK - EDGE, EDGE, 3 * EDGE, EDGE))
    jobs = []
    for pair in range(4):
        cut = lanes(pair)
        for group, (start, size, at, near) in enumerate(spans):
            rows = slice(start, start + size)
            keys = slice(group * KEYS, group * KEYS + near)

            def save(total, pair=pair, at=at, size=size):
                near_b[pair, at : at + size, :] = total

            jobs += attend_jobs(
                lambda rows=rows, cut=cut: qa[rows, cut],
                lambda at, keys=keys, cut=cut: kb[keys, cut][at],
                lambda at, keys=keys, cut=cut: vb[keys, cut][at],
                lambda rows=rows: own_f[rows, :],
                lambda at, keys=keys: f_kb[keys, :][at],
                save,
                whole=False,
            )
    pipelined(jobs, DEPTH_B)
    loads["spread"].wait()
    loads["tout_b"].wait()

    wait_all(feature_moves)
    edges_f = dot(spread[...], edge_f[...])
    column = lax.broadcasted_iota(jnp.int32, (EDGE, FEAT), 1)
    window_b = jnp.where(place < 36, 16, jnp.where(place < 72, 18, FEAT))
    ends = jnp.where(column == window_b, 1.0, 0.0)
    f_kb[EDGE : 2 * EDGE, :] = miss(halo_f[0:EDGE, :], after)
    f_kb[2 * KEYS + EDGE : 2 * KEYS + 2 * EDGE, :] = miss(halo_f[EDGE : 2 * EDGE, :], before)
    for group in range(3):
        region = edges_f[group * EDGE : (group + 1) * EDGE]
        f_kb[group * KEYS + 2 * EDGE : (group + 1) * KEYS, :] = miss(
            jnp.where(column < 16, region, ends)
        )
    wait_all(hidden_moves)
    halo[2 * EDGE :, :] = dot(spread[...], edge_in[...]).astype(BF)
    for ref, value in (
        (kb, keys_of(halo[...], w_b)),
        (vb, values_of(halo[...], w_b)),
    ):
        ref[EDGE : 2 * EDGE, :] = value[0:EDGE]
        ref[2 * KEYS + EDGE : 2 * KEYS + 2 * EDGE, :] = value[EDGE : 2 * EDGE]
        for group in range(3):
            at = (group + 2) * EDGE
            ref[group * KEYS + 2 * EDGE : (group + 1) * KEYS, :] = value[at : at + EDGE]

    jobs = []
    for pair in range(4):
        cut = lanes(pair)
        outs = []

        def done(out, _, outs=outs, cut=cut):
            outs.append(out)
            if len(outs) < 3:
                return
            first, second, third = outs
            upper = lax.broadcasted_iota(jnp.int32, (16, FEAT), 0) < 8
            att[0:64, cut] = first[0:64].astype(BF)
            att[64:80, cut] = jnp.where(upper, first[64:80], second[0:16]).astype(BF)
            att[80:208, cut] = second[16:144].astype(BF)
            att[208:224, cut] = jnp.where(upper, second[144:160], third[0:16]).astype(BF)
            att[224:288, cut] = third[16:80].astype(BF)

        for group, (start, size, at, near) in enumerate(spans):
            rows = slice(start, start + size)
            keys = slice(group * KEYS + near, (group + 1) * KEYS)
            jobs += attend_jobs(
                lambda rows=rows, cut=cut: qa[rows, cut],
                lambda at, keys=keys, cut=cut: kb[keys, cut][at],
                lambda at, keys=keys, cut=cut: vb[keys, cut][at],
                lambda rows=rows: own_f[rows, :],
                lambda at, keys=keys: f_kb[keys, :][at],
                done,
                lambda pair=pair, at=at, size=size: near_b[pair, at : at + size, :],
            )
    pipelined(jobs, DEPTH_B)


def backward_kernel(
    att, hid_t, pred, o_s, rq_s, rk_s, rd_s, q_s, k_s, v_s, att_s, exps_s,
    tout_b, sqkv, sout, sproj, heads,
    out_ref, grad_ref,
    da_s, dq_s, dk_s, dv_s,
):
    o = dot(att[...], tout_b[...])
    result = (hid_t[:, 0:512].astype(F32) + o * normed(o)).astype(BF)
    out_ref[...] = result
    residual = pred[...] - result.astype(F32)
    g = dot_nt(residual.astype(BF), sproj[...]).astype(BF).astype(F32)
    for layer in (1, 0):
        o = o_s[layer]
        scale = normed(o)
        y = o * scale
        d_o = scale * (g - y * jnp.mean(g * y, axis=-1, keepdims=True))
        da = dot_nt(d_o.astype(BF), sout[layer]).astype(BF)
        da_s[...] = (da.astype(F32) * rd_s[layer]).astype(BF)
        jobs = []
        for pair in range(2):
            for group in range(2):
                cut, rows = lanes(pair), rows_of(group)
                sums = []
                for half, mask in enumerate(pair_masks()):

                    def slope(rows=rows, cut=cut, mask=mask):
                        grad = da_s[rows, cut]
                        return dot_nt(
                            wide(v_s[layer, rows, cut] * mask, -mask),
                            wide(grad, grad * att_s[layer, rows, cut]),
                        )

                    def spread(slopes, rows=rows, cut=cut, mask=mask, sums=sums, at=layer * 4 + pair * 2 + half):
                        exps = exps_s[at, rows, :]
                        d_scores = exps * slopes.astype(BF)
                        parts = (
                            dot_tn(d_scores, k_s[layer, rows, cut] * mask),
                            dot(d_scores, q_s[layer, rows, cut] * mask),
                            dot(exps, da_s[rows, cut] * mask),
                        )
                        if not sums:
                            sums.append(parts)
                            return
                        dq, dk, dv = (one + two for one, two in zip(sums[0], parts))
                        dq_s[rows, cut] = dq
                        dk_s[rows, cut] = dk
                        dv_s[rows, cut] = dv.astype(BF)

                    jobs.append((slope, spread))
        pipelined(jobs, DEPTH_G)
        dq = dq_s[...] * SCALE
        q_hat = q_s[layer].astype(F32) * (1.0 / (SCALE * LOG2E))
        along = dot((q_hat * dq).astype(BF), heads[...])
        dq = (rq_s[layer] * (dq - q_hat * along)).astype(BF)
        dk = dk_s[...] * (1.0 / LOG2E)
        k_hat = k_s[layer].astype(F32)
        along = dot((k_hat * dk).astype(BF), heads[...])
        dk = (rk_s[layer] * (dk - k_hat * along)).astype(BF)
        w = sqkv.at[layer]
        g = g + (
            dot_nt(dq, w[:, 0:256])
            + dot_nt(dk, w[:, 256:512])
            + dot_nt(dv_s[...], w[:, 512:768])
        )
        if layer == 1:
            g = g.astype(BF).astype(F32)
    grad_ref[...] = g


def solution(mesh):
    n_lat, n_lon = mesh.shape["lat"], mesh.shape["lon"]

    def shards(teacher_in, student_in, regions, t_qkv, t_out, s_qkv, s_out, s_proj):
        assert teacher_in.shape == (1, ROWS, COLS, 512)
        vm = pl.BlockSpec(memory_space=pltpu.VMEM)
        hbm = pl.BlockSpec(memory_space=pltpu.HBM)
        state = [
            ((TOK, 512), BF),
            ((TOK, 512), BF),
            ((TOK, 512), F32),
            ((2, TOK, 256), F32),
            ((2, TOK, 256), F32),
            ((2, TOK, 256), F32),
            ((2, TOK, 256), F32),
            ((2, TOK, 256), BF),
            ((2, TOK, 256), BF),
            ((2, TOK, 256), BF),
            ((2, TOK, 256), BF),
            ((8, TOK, GROUP), BF),
            (t_out.shape[1:], BF),
            (s_qkv.shape, BF),
            (s_out.shape, BF),
            (s_proj.shape, BF),
            ((256, 256), BF),
        ]
        scratch = [
            ((TOK, 512), BF),
            ((TOK, 256), BF),
            ((COLS, 2, ROWS), jnp.int32),
            (t_qkv.shape, BF),
            (t_out.shape[1:], BF),
            ((PACK, GROUP), BF),
            ((KEYS, PACK), BF),
            ((4 * TOK, FEAT), BF),
            ((128, 128), F32),
            ((TOK, 512), BF),
            ((TOK, 512), BF),
            ((2, 2 * GROUP, 512), BF),
            ((2, 2 * GROUP, 512), BF),
            ((TOK, FEAT), BF),
            ((2, 2 * GROUP, FEAT), BF),
            ((TOK, 256), BF),
            ((PACK, 512), BF),
            ((PACK, 512), BF),
            ((HALO, 512), BF),
            ((3 * KEYS, 512), BF),
            ((3 * KEYS, 512), BF),
            ((3 * KEYS, FEAT), BF),
            ((TOK, FEAT), BF),
            ((PACK, FEAT), BF),
            ((PACK, FEAT), BF),
            ((2 * EDGE, FEAT), BF),
            ((4, 4 * EDGE, 256), F32),
        ]

        def columns_first(block):
            return block[0].transpose(1, 0, 2).reshape(TOK, block.shape[-1])

        def rows_first(block):
            return block.reshape(COLS, ROWS, block.shape[-1]).transpose(1, 0, 2)[None]

        def shapes(entries):
            return tuple(jax.ShapeDtypeStruct(shape, kind) for shape, kind in entries)

        def buffers(entries):
            return [pltpu.VMEM(shape, kind) for shape, kind in entries]

        operands = (
            columns_first(teacher_in),
            columns_first(student_in),
            regions.transpose(2, 0, 1),
            t_qkv,
            t_out,
            s_qkv,
            s_out,
            s_proj,
        ) + constants()
        operands = tuple(
            pltpu.with_memory_space_constraint(operand, pltpu.HBM) for operand in operands
        )
        saved = pl.pallas_call(
            functools.partial(forward_kernel, n_lat, n_lon),
            out_shape=shapes(state),
            in_specs=[hbm] * len(operands),
            out_specs=(vm,) * len(state),
            scratch_shapes=buffers(scratch)
            + [pltpu.SemaphoreType.DMA((count,)) for count in (14, 21, 21)],
            compiler_params=pltpu.CompilerParams(
                collective_id=0, has_side_effects=True, vmem_limit_bytes=K1_VMEM
            ),
            name="forward",
        )(*operands)
        teacher_out, grad = pl.pallas_call(
            backward_kernel,
            out_shape=shapes((((TOK, 512), BF), ((TOK, 256), F32))),
            in_specs=[vm] * len(saved),
            out_specs=(vm, vm),
            scratch_shapes=buffers(
                (((TOK, 256), BF), ((TOK, 256), F32), ((TOK, 256), F32), ((TOK, 256), BF))
            ),
            compiler_params=pltpu.CompilerParams(vmem_limit_bytes=K2_VMEM),
            name="backward",
        )(*saved)
        return rows_first(teacher_out), rows_first(grad)

    return jax.shard_map(
        shards,
        mesh=mesh,
        in_specs=(
            P("grp", "lat", "lon", None),
            P("grp", "lat", "lon", None),
            P(None, "lat", "lon"),
            P(),
            P(),
            P(),
            P(),
            P(),
        ),
        out_specs=(P("grp", "lat", "lon", None), P("grp", "lat", "lon", None)),
        check_vma=False,
    )
```
